32 devices in a mesh: parts: 1, seq: 32 (over z, y, x, core).
Axes of the slice: x: 2, y: 2, z: 4, core: 2. Of those that a mesh axis runs over, the one named last changes fastest.
Arguments:
- tokens: bfloat16 [1, 128, 3, 128, 3072], P('parts', 'seq'), may hold values from -6 to 6
- queries: bfloat16 [1, 128, 3, 128, 1536], P('parts', 'seq'), may hold values from -68 to 68
- key_weight: bfloat16 [3072, 1536], P('seq'), may hold values from -0.109375 to 0.109375
- value_weight: bfloat16 [3072, 1536], P('seq'), may hold values from -0.109375 to 0.109375
- halves: int32 [1, 128, 3, 2, 2], P('parts', 'seq'), may hold values from 1 to 3
Outputs:
- mixed: bfloat16 [1, 128, 3, 128, 1536], P('parts', 'seq')
The draws below stay inside these ranges and needn't reach their ends.
Inputs may be any that keep to these rules, and one draw needn't show every extreme that they name: `halves`: 1 lists the first half of the partner lines, 2 the second half, 3 both.
All inputs are finite; a program needn't handle non-finite values.
Results may differ from the reference program's by a relative error of at most 0.012.
Values may be sent and summed in bfloat16 or wider, within the bound.
No kernel may reach another device: no remote copies, remote signals or barrier semaphores. Data moves between devices by JAX's collectives and lax.ppermute only.
A program may use at most 128 MiB of HBM per device.

```python
import math
import jax
import jax.numpy as jnp
from jax import lax

D = 3072
HEADS = 12
HDIM = 128
RES = 128
SCENES = 1
HW = 1536


def draw_queries(key, part):
    full_shape = (SCENES, RES, 3, RES, HEADS * HDIM)
    key_values = jax.random.fold_in(key, 0)
    drawn = jnp.clip(jax.random.normal(key_values, full_shape, jnp.float32), -6.0, 6.0)
    return drawn.astype(jnp.bfloat16)


def place_ends(result, rng, smallest, high):
    longest = result.shape.index(max(result.shape))
    spots = []
    for shift in (0, 1):
        where = [jax.random.randint(jax.random.fold_in(rng, axis), (), 0, length) for axis, length in enumerate(result.shape)]
        where[longest] = (where[longest] + shift) % result.shape[longest]
        spots.append(tuple(where))
    return result.at[spots[0]].set(smallest).at[spots[1]].set(high)


def shard_levels(own_key, shape, pieces, least, high):
    loudness, own = 1.0, jax.random.fold_in(own_key, 6)
    for position, blocks in pieces:
        steps = jnp.exp(jax.random.uniform(jax.random.fold_in(own, position), (blocks,), jnp.float32, least / len(pieces), high / len(pieces)))
        loudness = loudness * jnp.repeat(steps, shape[position] // blocks).reshape([-1 if axis == position else 1 for axis in range(len(shape))])
    return loudness


def scatter_about(rng, dims, spread, bound, cuts=(), kind=jnp.bfloat16):
    entries = spread * jax.random.normal(rng, dims, jnp.float32)
    if cuts:
        entries = entries * shard_levels(rng, dims, cuts, -0.22, 0.18)
    return jnp.clip(entries, -bound, bound).astype(kind)


def setup_inputs(seed: int = 0, part: int = 0) -> dict:
    key_of = jax.random.split(jax.random.key(seed), 6)
    part_splits = jax.random.split(jax.random.fold_in(key_of[5], part), 6)
    tokens = scatter_about(part_splits[0], (SCENES, RES, 3, RES, D), 1.0, 6.0, ((1, 32),))
    queries = draw_queries(jax.random.fold_in(jax.random.fold_in(key_of[5], part), 71), part)
    key_weight = scatter_about(key_of[2], (D, HW), D ** -0.5, 0.109375, ((0, 32),))
    value_weight = scatter_about(key_of[3], (D, HW), D ** -0.5, 0.109375, ((0, 32),))
    halves = place_ends(jax.random.randint(part_splits[4], (SCENES, RES, 3, 2, 2), 1, 4), jax.random.fold_in(part_splits[4], 1), 1, 3).astype(jnp.int32)
    return {"tokens": tokens, "queries": queries, "key_weight": key_weight, "value_weight": value_weight, "halves": halves}


def kept_keys(code_grid):
    column = jnp.arange(RES)
    first_kept = (code_grid % 2 == 1)[..., None]
    second_kept = (code_grid >= 2)[..., None]
    return jnp.where(column < RES // 2, first_kept, second_kept)[..., None, :]

def partial_attention(queries_h, keys_h, values_h, score_form, value_form, kept_mask):
    scores = jnp.einsum(score_form, queries_h, keys_h) * (1.0 / math.sqrt(HDIM))
    masked = jnp.where(kept_mask, scores, -jnp.inf)
    peak_val = lax.optimization_barrier(jnp.max(masked, axis=-1))
    weights = jnp.exp(masked - peak_val[..., None])
    totals = lax.optimization_barrier(jnp.sum(weights, axis=-1))
    rounded = lax.optimization_barrier(weights.astype(jnp.bfloat16)).astype(jnp.float32)
    partial_out = jnp.einsum(value_form, rounded, values_h)
    return (partial_out, peak_val, totals)

def merge_slots(near_part, far_part):
    far_mean = lax.optimization_barrier((far_part[0] / far_part[2][..., None]).astype(jnp.bfloat16)).astype(jnp.float32)
    peak_val = jnp.maximum(near_part[1], far_part[1])
    near_w = jnp.exp(near_part[1] - peak_val)
    far_w = jnp.exp(far_part[1] - peak_val) * far_part[2]
    upper = near_part[0] * near_w[..., None] + far_mean * far_w[..., None]
    return upper / (near_part[2] * near_w + far_w)[..., None]

def reference(tokens, queries, key_weight, value_weight, halves):
    half_index = jnp.arange(RES) // (RES // 2)
    slot_plan = (((1, 'abhd,ajhd->abhj', 'abhj,ajhd->abhd'), (2, 'abhd,bjhd->abhj', 'abhj,bjhd->abhd')), ((0, 'abhd,ajhd->abhj', 'abhj,ajhd->abhd'), (2, 'abhd,jbhd->abhj', 'abhj,jbhd->abhd')), ((0, 'abhd,jahd->abhj', 'abhj,jahd->abhd'), (1, 'abhd,jbhd->abhj', 'abhj,jbhd->abhd')))
    scene_outs = []
    for scene_idx in range(SCENES):
        flat_rows = tokens[scene_idx].reshape(-1, D)
        keys_all = jnp.dot(flat_rows, key_weight, preferred_element_type=jnp.float32).astype(jnp.bfloat16)
        keys_all = keys_all.reshape(RES, 3, RES, HEADS, HDIM).astype(jnp.float32)
        values_all = jnp.dot(flat_rows, value_weight, preferred_element_type=jnp.float32).astype(jnp.bfloat16)
        values_all = values_all.reshape(RES, 3, RES, HEADS, HDIM).astype(jnp.float32)
        query_all = queries[scene_idx].reshape(RES, 3, RES, HEADS, HDIM).astype(jnp.float32)
        plane_outs = []
        for plane_idx in range(3):
            results = []
            for slot_idx in range(2):
                source_idx, score_form, value_form = slot_plan[plane_idx][slot_idx]
                code_pairs = halves[scene_idx, :, plane_idx, :, slot_idx]
                code_grid = jnp.where(half_index[None, :] == 0, code_pairs[:, 0:1], code_pairs[:, 1:2])
                results.append(partial_attention(query_all[:, plane_idx], keys_all[:, source_idx], values_all[:, source_idx], score_form, value_form, kept_keys(code_grid)))
            merged = merge_slots(results[0], results[1])
            plane_outs.append(merged.reshape(RES, RES, HEADS * HDIM))
        scene_outs.append(jnp.stack(plane_outs, axis=1).astype(jnp.bfloat16))
    return jnp.stack(scene_outs, axis=0)
```

```python
import functools
import math

import jax
import jax.numpy as jnp
import numpy as np
from jax import lax
from jax.experimental import pallas as pl
from jax.experimental.pallas import tpu as pltpu
from jax.sharding import PartitionSpec as P

HEADS = 12
HDIM = 128
LANES = 128
SCALE = 1.0 / math.sqrt(HDIM)
BF16 = jnp.bfloat16
F32 = jnp.float32


def home_order(lines, res):
    span = res // lines
    out = np.zeros((res, res), np.float32)
    for line in range(lines):
        for dest in range(span // lines):
            for pos in range(lines):
                out[(dest * lines + pos) * lines + line, line * span + dest * lines + pos] = 1.0
    return out


def away_order(lines, res):
    span = res // lines
    out = np.zeros((res, res), np.float32)
    for src in range(span // lines):
        for pos in range(lines):
            for line in range(lines):
                out[pos * span + src * lines + line, (src * lines + pos) * lines + line] = 1.0
    return out


def pick(order, rows):
    return jnp.dot(order, rows, preferred_element_type=F32).astype(BF16)


def order_kernel(x_ref, order_ref, out_ref):
    lines, span, width = x_ref.shape
    out_ref[...] = pick(order_ref[...], x_ref[...].reshape(lines * span, width))


def order_queries(queries, order):
    lines, planes, res, width = queries.shape
    span = res // lines
    return pl.pallas_call(
        order_kernel,
        grid=(planes, lines),
        in_specs=[
            pl.BlockSpec((lines, None, span, width), lambda p, i: (0, p, i, 0)),
            pl.BlockSpec((res, res), lambda p, i: (0, 0)),
        ],
        out_specs=pl.BlockSpec((res, width), lambda p, i: (i, p)),
        out_shape=jax.ShapeDtypeStruct((lines * res, planes * width), BF16),
        cost_estimate=pl.CostEstimate(
            flops=2 * queries.size * res, bytes_accessed=4 * queries.size, transcendentals=0
        ),
        name="order_queries",
    )(queries, order)


def project_kernel(x_ref, w_ref, order_ref, home_ref, sent_ref):
    lines, res, depth = x_ref.shape
    tile = w_ref.shape[1]
    span = res // lines
    out = jnp.dot(x_ref[...].reshape(lines * res, depth), w_ref[...], preferred_element_type=F32)
    out = out.astype(BF16).reshape(lines, res, tile)
    home_ref[...] = out
    for i in range(lines):
        rows = out[:, i * span : (i + 1) * span].reshape(res, tile)
        sent_ref[pl.ds(i * res, res), :] = pick(order_ref[...], rows)


def project(tokens, weight, order, plane):
    lines, planes, res, depth = tokens.shape
    width = weight.shape[1]
    tile = 256
    return pl.pallas_call(
        project_kernel,
        grid=(width // tile,),
        in_specs=[
            pl.BlockSpec((lines, None, res, depth), lambda n: (0, plane, 0, 0)),
            pl.BlockSpec((depth, tile), lambda n: (0, n)),
            pl.BlockSpec((res, res), lambda n: (0, 0)),
        ],
        out_specs=[
            pl.BlockSpec((lines, res, tile), lambda n: (0, 0, n)),
            pl.BlockSpec((lines * res, tile), lambda n: (0, n)),
        ],
        out_shape=[
            jax.ShapeDtypeStruct((lines, res, width), BF16),
            jax.ShapeDtypeStruct((lines * res, width), BF16),
        ],
        cost_estimate=pl.CostEstimate(
            flops=2 * lines * res * depth * width,
            bytes_accessed=2 * (lines * res * (depth + 2 * width) + depth * width),
            transcendentals=0,
        ),
        name=f"project_{plane}",
    )(tokens, weight, order)


def to_away(src_ref, order_ref, dst_ref):
    lines, res, width = dst_ref.shape
    span = res // lines
    for c in range(lines):
        rows = pick(order_ref[...], src_ref[pl.ds(c * res, res), :])
        for pos in range(lines):
            dst_ref[pos, pl.ds(c * span, span), :] = rows[pos * span : (pos + 1) * span]


def attend(q, k, v, bias):
    scores = lax.dot_general(q, k, (((1,), (1,)), ((), ())), preferred_element_type=F32)
    scores = scores * SCALE + bias
    peak = jnp.max(scores, axis=1, keepdims=True)
    weights = jnp.exp(scores - peak)
    total = jnp.sum(weights, axis=1, keepdims=True)
    out = jnp.dot(weights.astype(BF16), v, preferred_element_type=F32)
    return out, peak, total


def far_kernel(moved_kv, q_ref, kv_ref, bias_ref, order_ref, back_ref, out_ref, q_s, kv_s, mean_s):
    lines, res, width = q_s.shape
    span = res // lines
    heads = width // HDIM
    to_away(q_ref, order_ref, q_s)
    if moved_kv:
        to_away(kv_ref, order_ref, kv_s)
    else:
        kv_s = kv_ref
    lane = lax.broadcasted_iota(jnp.int32, (res, LANES), 1)

    def step(i, carry):
        lse = jnp.zeros((res, LANES), F32)
        for h in range(heads):
            at = pl.ds(h * HDIM, HDIM)
            out, peak, total = attend(
                q_s[i, :, at], kv_s[i, :, at], kv_s[i, :, pl.ds(width + h * HDIM, HDIM)], bias_ref[...]
            )
            mean_s[i, :, at] = (out * (1.0 / total)).astype(BF16)
            lse = jnp.where(lane == h, peak + jnp.log(total), lse)
        high = lse.astype(BF16).astype(F32)
        mid = (lse - high).astype(BF16).astype(F32)
        low = (lse - high - mid).astype(BF16).astype(F32)
        parts = high + pltpu.roll(mid, 16, 1) + pltpu.roll(low, 32, 1)
        mean_s[i, :, pl.ds(width, LANES)] = parts.astype(BF16)
        return carry

    lax.fori_loop(0, lines, step, 0)
    for c in range(lines):
        rows = jnp.concatenate([mean_s[pos, pl.ds(c * span, span), :] for pos in range(lines)], axis=0)
        out_ref[pl.ds(c * res, res), :] = pick(back_ref[...], rows)


VMEM_SPEC = pl.BlockSpec(memory_space=pltpu.VMEM)


def attention_cost(lines, res, width):
    return pl.CostEstimate(
        flops=4 * lines * res * res * width,
        bytes_accessed=2 * lines * res * width * 5,
        transcendentals=lines * res * res * (width // HDIM),
    )


def far_attention(moved_q, kv, bias, order, back, plane, lines, res, width):
    moved_kv = kv.ndim == 2
    kv_shape = (lines, res, 2 * width) if moved_kv else (1, 16, LANES)
    return pl.pallas_call(
        functools.partial(far_kernel, moved_kv),
        grid=(1,),
        in_specs=[
            pl.BlockSpec((lines * res, width), lambda n: (0, plane)),
            pl.BlockSpec(kv.shape, lambda n: (0,) * kv.ndim),
            pl.BlockSpec((None, res, res), lambda n: (plane, 0, 0)),
            pl.BlockSpec((res, res), lambda n: (0, 0)),
            pl.BlockSpec((res, res), lambda n: (0, 0)),
        ],
        out_specs=pl.BlockSpec((lines * res, width + LANES), lambda n: (0, 0)),
        out_shape=jax.ShapeDtypeStruct((lines * res, width + LANES), BF16),
        scratch_shapes=[
            pltpu.VMEM((lines, res, width), BF16),
            pltpu.VMEM(kv_shape, BF16),
            pltpu.VMEM((lines, res, width + LANES), BF16),
        ],
        cost_estimate=attention_cost(lines, res, width),
        name=f"far_{plane}",
    )(moved_q, kv, bias, order, back)


def near_kernel(moved_kv, q_ref, kv_ref, bias_ref, far_ref, order_ref, back_ref, done_ref, out_ref, kv_s, far_s):
    lines, res, width = q_ref.shape
    span = res // lines
    heads = width // HDIM
    if moved_kv:
        to_away(kv_ref, order_ref, kv_s)
    else:
        kv_s = kv_ref
    for c in range(lines):
        rows = pick(back_ref[...], far_ref[pl.ds(c * res, res), :])
        for line in range(lines):
            far_s[line, pl.ds(c * span, span), :] = rows[line * span : (line + 1) * span]

    def step(i, carry):
        parts = far_s[i, :, pl.ds(width, LANES)].astype(F32)
        lse = parts + pltpu.roll(parts, LANES - 16, 1) + pltpu.roll(parts, LANES - 32, 1)
        for h in range(heads):
            at = pl.ds(h * HDIM, HDIM)
            out, peak, total = attend(
                q_ref[i, :, at], kv_s[i, :, at], kv_s[i, :, pl.ds(width + h * HDIM, HDIM)], bias_ref[i]
            )
            far_lse = lse[:, h : h + 1]
            top = jnp.maximum(peak, far_lse)
            near_w = jnp.exp(peak - top)
            far_w = jnp.exp(far_lse - top)
            scale = 1.0 / (total * near_w + far_w)
            mixed = out * (near_w * scale) + far_s[i, :, at].astype(F32) * (far_w * scale)
            out_ref[i, :, at] = mixed.astype(BF16)
        return carry

    lax.fori_loop(0, lines, step, 0)


def near_attention(queries, kv, bias, far, order, back, plane, done):
    lines, planes, res, width = queries.shape
    moved_kv = kv.ndim == 2
    kv_shape = (lines, res, 2 * width) if moved_kv else (1, 16, LANES)
    first = done is None
    kernel = functools.partial(near_kernel, moved_kv)
    in_specs = [
        pl.BlockSpec((lines, None, res, width), lambda n: (0, plane, 0, 0)),
        pl.BlockSpec(kv.shape, lambda n: (0,) * kv.ndim),
        pl.BlockSpec((None, lines, res, res), lambda n: (plane, 0, 0, 0)),
        pl.BlockSpec((lines * res, width + LANES), lambda n: (0, 0)),
        pl.BlockSpec((res, res), lambda n: (0, 0)),
        pl.BlockSpec((res, res), lambda n: (0, 0)),
        pl.BlockSpec(memory_space=pl.ANY),
    ]
    args = (queries, kv, bias, far, order, back)
    if first:
        body = lambda *refs: kernel(*refs[:6], None, *refs[6:])
        in_specs = in_specs[:-1]
        alias = {}
    else:
        body = kernel
        args = args + (done,)
        alias = {6: 0}
    return pl.pallas_call(
        body,
        grid=(1,),
        in_specs=in_specs,
        out_specs=pl.BlockSpec((lines, None, res, width), lambda n: (0, plane, 0, 0)),
        out_shape=jax.ShapeDtypeStruct(queries.shape, BF16),
        scratch_shapes=[
            pltpu.VMEM(kv_shape, BF16),
            pltpu.VMEM((lines, res, width + LANES), BF16),
        ],
        input_output_aliases=alias,
        cost_estimate=attention_cost(lines, res, width),
        name=f"near_{plane}",
    )(*args)


def mask_bias(codes, res):
    first_kept = (codes % 2 == 1)[..., None]
    second_kept = (codes >= 2)[..., None]
    kept = jnp.where(jnp.arange(res) < res // 2, first_kept, second_kept)
    return jnp.where(kept, 0.0, -jnp.inf).astype(F32)


def exchange(rows):
    return lax.all_to_all(rows, "seq", split_axis=0, concat_axis=0, tiled=True)


def on_device(count, tokens, queries, key_weight, value_weight, halves):
    scenes, lines, planes, res, depth = tokens.shape
    width = queries.shape[-1]
    tokens = tokens.reshape(lines, planes, res, depth)
    queries = queries.reshape(lines, planes, res, width)
    halves = halves.reshape(lines, planes, 2, 2)
    to_sent = jnp.asarray(home_order(lines, res), BF16)
    to_home = jnp.asarray(home_order(lines, res).T, BF16)
    away = jnp.asarray(away_order(lines, res), BF16)
    from_away = jnp.asarray(away_order(lines, res).T, BF16)

    weight = lax.all_gather(jnp.concatenate([key_weight, value_weight], axis=1), "seq", axis=0, tiled=True)

    dest_half = (np.arange(count) * lines) // (res // 2)
    sent_codes = jnp.where(
        (dest_half == 0)[:, None], halves[:, :, 0, 1].reshape(1, -1), halves[:, :, 1, 1].reshape(1, -1)
    )
    codes = exchange(sent_codes).reshape(res, planes).T
    far_bias = mask_bias(codes, res)
    home_half = jnp.arange(res) // (res // 2)
    near_codes = jnp.where(home_half == 0, halves[:, :, 0:1, 0], halves[:, :, 1:2, 0])
    near_bias = mask_bias(near_codes.transpose(1, 0, 2), res)

    moved_q = exchange(order_queries(queries, to_sent))
    home_2, sent_2 = project(tokens, weight, to_sent, 2)
    moved_2 = exchange(sent_2)
    home_1, sent_1 = project(tokens, weight, to_sent, 1)
    far = functools.partial(far_attention, order=away, back=from_away, lines=lines, res=res, width=width)
    far_0 = exchange(far(moved_q, home_2, far_bias, plane=0))
    moved_1 = exchange(sent_1)
    home_0, sent_0 = project(tokens, weight, to_sent, 0)
    far_1 = exchange(far(moved_q, moved_2, far_bias, plane=1))
    moved_0 = exchange(sent_0)
    far_2 = exchange(far(moved_q, moved_1, far_bias, plane=2))
    out = near_attention(queries, home_1, near_bias, far_0, away, to_home, 0, None)
    out = near_attention(queries, home_0, near_bias, far_1, away, to_home, 1, out)
    out = near_attention(queries, moved_0, near_bias, far_2, away, to_home, 2, out)
    return out.reshape(scenes, lines, planes, res, width)


def solution(mesh):
    in_specs = (
        P("parts", "seq", None, None, None),
        P("parts", "seq", None, None, None),
        P("seq", None),
        P("seq", None),
        P("parts", "seq", None, None, None),
    )
    return jax.shard_map(
        functools.partial(on_device, mesh.shape["seq"]),
        mesh=mesh,
        in_specs=in_specs,
        out_specs=P("parts", "seq", None, None, None),
        check_vma=False,
    )
```

```python
import functools
import math

import jax
import jax.numpy as jnp
import numpy as np
from jax import lax
from jax.experimental import pallas as pl
from jax.experimental.pallas import tpu as pltpu
from jax.sharding import PartitionSpec as P

HEADS = 12
HDIM = 128
LANES = 128
PLANES = 3
SCALE = 1.0 / math.sqrt(HDIM)
BF16 = jnp.bfloat16
F32 = jnp.float32


def home_order(lines, res):
    span = res // lines
    out = np.zeros((res, res), np.float32)
    for line in range(lines):
        for dest in range(span // lines):
            for pos in range(lines):
                out[(dest * lines + pos) * lines + line, line * span + dest * lines + pos] = 1.0
    return out


def away_order(lines, res):
    span = res // lines
    out = np.zeros((res, res), np.float32)
    for src in range(span // lines):
        for pos in range(lines):
            for line in range(lines):
                out[pos * span + src * lines + line, (src * lines + pos) * lines + line] = 1.0
    return out


def pick(order, rows):
    return jnp.dot(order, rows, preferred_element_type=F32).astype(BF16)


def order_kernel(tokens_ref, queries_ref, order_ref, out_ref):
    lines, res, width = queries_ref.shape
    span = res // lines
    first = pl.program_id(0) < pl.num_programs(0) - PLANES

    def put(ref):
        for i in range(lines):
            rows = ref[:, pl.ds(i * span, span), :].reshape(res, width)
            out_ref[pl.ds(i * res, res), :] = pick(order_ref[...], rows)

    pl.when(first)(lambda: put(tokens_ref))
    pl.when(jnp.logical_not(first))(lambda: put(queries_ref))


def order_sent(tokens, queries, order):
    lines, planes, res, width = queries.shape
    depth = tokens.shape[-1]
    lead = depth // width
    return pl.pallas_call(
        order_kernel,
        grid=(lead + planes,),
        in_specs=[
            pl.BlockSpec((lines, None, res, width), lambda p: (0, 0, 0, jnp.minimum(p, lead - 1))),
            pl.BlockSpec((lines, None, res, width), lambda p: (0, jnp.maximum(p - lead, 0), 0, 0)),
            pl.BlockSpec((res, res), lambda p: (0, 0)),
        ],
        out_specs=pl.BlockSpec((lines * res, width), lambda p: (0, p)),
        out_shape=jax.ShapeDtypeStruct((lines * res, depth + planes * width), BF16),
        cost_estimate=pl.CostEstimate(
            flops=2 * lines * res * (depth + planes * width) * res,
            bytes_accessed=4 * lines * res * (depth + planes * width),
            transcendentals=0,
        ),
        name="order_sent",
    )(tokens, queries, order)


def project_kernel(x_ref, w_ref, order_ref, *out_refs):
    out = jnp.dot(x_ref[...].reshape(-1, x_ref.shape[-1]), w_ref[...], preferred_element_type=F32)
    out = out.astype(BF16)
    tile = w_ref.shape[1]
    home_ref = out_refs[0]
    home_ref[...] = out.reshape(home_ref.shape)
    if len(out_refs) > 1:
        lines, res, _ = x_ref.shape
        span = res // lines
        by_line = out.reshape(lines, res, tile)
        for i in range(lines):
            rows = by_line[:, i * span : (i + 1) * span].reshape(res, tile)
            out_refs[1][pl.ds(i * res, res), :] = pick(order_ref[...], rows)


def project(tokens, weight, order, plane, sent_width):
    depth, width = weight.shape
    tile = 512
    if tokens.ndim == 4:
        lines, planes, res, _ = tokens.shape
        x_spec = pl.BlockSpec((lines, None, res, depth), lambda n: (0, plane, 0, 0))
        rows = lines * res
        out_specs = [pl.BlockSpec((lines, res, tile), lambda n: (0, 0, n))]
        out_shape = [jax.ShapeDtypeStruct((lines, res, width), BF16)]
    else:
        rows = tokens.shape[0]
        x_spec = pl.BlockSpec((rows, depth), lambda n: (0, 0))
        out_specs = [pl.BlockSpec((rows, tile), lambda n: (0, n))]
        out_shape = [jax.ShapeDtypeStruct((rows, width), BF16)]
    if sent_width:
        out_specs.append(pl.BlockSpec((rows, tile), lambda n: (0, n)))
        out_shape.append(jax.ShapeDtypeStruct((rows, sent_width), BF16))
    return pl.pallas_call(
        project_kernel,
        grid=(width // tile,),
        in_specs=[
            x_spec,
            pl.BlockSpec((depth, tile), lambda n: (0, n)),
            pl.BlockSpec(order.shape, lambda n: (0, 0)),
        ],
        out_specs=out_specs,
        out_shape=out_shape,
        cost_estimate=pl.CostEstimate(
            flops=2 * rows * depth * width,
            bytes_accessed=2 * (rows * (depth + 2 * width) + depth * width),
            transcendentals=0,
        ),
        name=f"project_{plane}",
    )(tokens, weight, order)


def to_away(src_ref, order_ref, dst_ref):
    lines, res, width = dst_ref.shape
    span = res // lines
    for c in range(lines):
        rows = pick(order_ref[...], src_ref[pl.ds(c * res, res), :])
        for pos in range(lines):
            dst_ref[pos, pl.ds(c * span, span), :] = rows[pos * span : (pos + 1) * span]


def attend(q, k, v, bias):
    scores = lax.dot_general(q, k, (((1,), (1,)), ((), ())), preferred_element_type=F32)
    scores = scores * SCALE + bias
    peak = jnp.max(scores, axis=1, keepdims=True)
    weights = jnp.exp(scores - peak)
    total = jnp.sum(weights, axis=1, keepdims=True)
    out = jnp.dot(weights.astype(BF16), v, preferred_element_type=F32)
    return out, peak, total


def far_kernel(moved_kv, column, q_ref, kv_ref, bias_ref, order_ref, back_ref, *rest):
    out_ref, q_s, kv_s, mean_s, sent_s, sem = rest[-6:]
    lines, res, width = q_s.shape
    span = res // lines
    heads = width // HDIM
    to_away(q_ref, order_ref, q_s)
    if moved_kv:
        to_away(kv_ref, order_ref, kv_s)
    else:
        kv_s = kv_ref
    lane = lax.broadcasted_iota(jnp.int32, (res, LANES), 1)

    def step(i, carry):
        lse = jnp.zeros((res, LANES), F32)
        for h in range(heads):
            at = pl.ds(h * HDIM, HDIM)
            out, peak, total = attend(
                q_s[i, :, at], kv_s[i, :, at], kv_s[i, :, pl.ds(width + h * HDIM, HDIM)], bias_ref[...]
            )
            mean_s[i, :, at] = (out * (1.0 / total)).astype(BF16)
            lse = jnp.where(lane == h, peak + jnp.log(total), lse)
        high = lse.astype(BF16).astype(F32)
        mid = (lse - high).astype(BF16).astype(F32)
        low = (lse - high - mid).astype(BF16).astype(F32)
        parts = high + pltpu.roll(mid, 16, 1) + pltpu.roll(low, 32, 1)
        mean_s[i, :, pl.ds(width, LANES)] = parts.astype(BF16)
        return carry

    lax.fori_loop(0, lines, step, 0)
    for c in range(lines):
        rows = jnp.concatenate([mean_s[pos, pl.ds(c * span, span), :] for pos in range(lines)], axis=0)
        sent_s[pl.ds(c * res, res), :] = pick(back_ref[...], rows)
    copy = pltpu.make_async_copy(sent_s, out_ref.at[:, pl.ds(column, width + LANES)], sem)
    copy.start()
    copy.wait()


VMEM_SPEC = pl.BlockSpec(memory_space=pltpu.VMEM)


def attention_cost(lines, res, width):
    return pl.CostEstimate(
        flops=4 * lines * res * res * width,
        bytes_accessed=2 * lines * res * width * 5,
        transcendentals=lines * res * res * (width // HDIM),
    )


def far_attention(moved_q, kv, bias, order, back, plane, lead, lines, res, width, into=None):
    moved_kv = kv.ndim == 2
    kv_shape = (lines, res, 2 * width) if moved_kv else (1, 16, LANES)
    kv_block = kv.shape[:-1] + (2 * width,)
    column = 0 if into is None else into.shape[1] - width - LANES
    shape = (lines * res, column + width + LANES)
    in_specs = [
        pl.BlockSpec((lines * res, width), lambda n: (0, lead + plane)),
        pl.BlockSpec(kv_block, lambda n: (0,) * kv.ndim),
        pl.BlockSpec((None, res, res), lambda n: (plane, 0, 0)),
        pl.BlockSpec((res, res), lambda n: (0, 0)),
        pl.BlockSpec((res, res), lambda n: (0, 0)),
    ]
    args = (moved_q, kv, bias, order, back)
    if into is not None:
        in_specs.append(pl.BlockSpec(memory_space=pl.ANY))
        args = args + (into,)
    return pl.pallas_call(
        functools.partial(far_kernel, moved_kv, column),
        grid=(1,),
        in_specs=in_specs,
        out_specs=pl.BlockSpec(memory_space=pl.ANY),
        out_shape=jax.ShapeDtypeStruct(shape, BF16),
        scratch_shapes=[
            pltpu.VMEM((lines, res, width), BF16),
            pltpu.VMEM(kv_shape, BF16),
            pltpu.VMEM((lines, res, width + LANES), BF16),
            pltpu.VMEM((lines * res, width + LANES), BF16),
            pltpu.SemaphoreType.DMA,
        ],
        input_output_aliases={} if into is None else {5: 0},
        cost_estimate=attention_cost(lines, res, width),
        name=f"far_{plane}",
    )(*args)


def far_sum(parts):
    return parts + pltpu.roll(parts, LANES - 16, 1) + pltpu.roll(parts, LANES - 32, 1)


def near_kernel(column, q_ref, kv_ref, bias_ref, far_ref, back_ref, *rest):
    out_ref, far_s = rest[-2:]
    lines, res, width = q_ref.shape
    span = res // lines
    heads = width // HDIM
    for c in range(lines):
        rows = pick(back_ref[...], far_ref[pl.ds(c * res, res), pl.ds(column, width + LANES)])
        for line in range(lines):
            far_s[line, pl.ds(c * span, span), :] = rows[line * span : (line + 1) * span]

    def step(i, carry):
        lse = far_sum(far_s[i, :, pl.ds(width, LANES)].astype(F32))
        for h in range(heads):
            at = pl.ds(h * HDIM, HDIM)
            out, peak, total = attend(
                q_ref[i, :, at], kv_ref[i, :, at], kv_ref[i, :, pl.ds(width + h * HDIM, HDIM)], bias_ref[i]
            )
            far_lse = lse[:, h : h + 1]
            top = jnp.maximum(peak, far_lse)
            near_w = jnp.exp(peak - top)
            far_w = jnp.exp(far_lse - top)
            scale = 1.0 / (total * near_w + far_w)
            mixed = out * (near_w * scale) + far_s[i, :, at].astype(F32) * (far_w * scale)
            out_ref[i, :, at] = mixed.astype(BF16)
        return carry

    lax.fori_loop(0, lines, step, 0)


def near_attention(queries, kv, bias, far, back, plane, done):
    lines, planes, res, width = queries.shape
    in_specs = [
        pl.BlockSpec((lines, None, res, width), lambda n: (0, plane, 0, 0)),
        pl.BlockSpec(kv.shape, lambda n: (0,) * kv.ndim),
        pl.BlockSpec((None, lines, res, res), lambda n: (plane, 0, 0, 0)),
        pl.BlockSpec(far.shape, lambda n: (0, 0)),
        pl.BlockSpec((res, res), lambda n: (0, 0)),
    ]
    args = (queries, kv, bias, far, back)
    if done is not None:
        in_specs.append(pl.BlockSpec(memory_space=pl.ANY))
        args = args + (done,)
    return pl.pallas_call(
        functools.partial(near_kernel, far.shape[1] - width - LANES),
        grid=(1,),
        in_specs=in_specs,
        out_specs=pl.BlockSpec((lines, None, res, width), lambda n: (0, plane, 0, 0)),
        out_shape=jax.ShapeDtypeStruct(queries.shape, BF16),
        scratch_shapes=[pltpu.VMEM((lines, res, width + LANES), BF16)],
        input_output_aliases={} if done is None else {5: 0},
        cost_estimate=attention_cost(lines, res, width),
        name=f"near_{plane}",
    )(*args)


def part_kernel(q_ref, kv_ref, bias_ref, order_ref, mean_ref, lse_ref, kv_s):
    lines, res, width = q_ref.shape
    heads = width // HDIM
    to_away(kv_ref, order_ref, kv_s)
    lane = lax.broadcasted_iota(jnp.int32, (res, LANES), 1)

    def step(i, carry):
        lse = jnp.zeros((res, LANES), F32)
        for h in range(heads):
            at = pl.ds(h * HDIM, HDIM)
            out, peak, total = attend(
                q_ref[i, :, at], kv_s[i, :, at], kv_s[i, :, pl.ds(width + h * HDIM, HDIM)], bias_ref[i]
            )
            mean_ref[i, :, at] = out * (1.0 / total)
            lse = jnp.where(lane == h, peak + jnp.log(total), lse)
        lse_ref[i] = lse
        return carry

    lax.fori_loop(0, lines, step, 0)


def near_part(queries, kv, bias, order, plane):
    lines, planes, res, width = queries.shape
    return pl.pallas_call(
        part_kernel,
        grid=(1,),
        in_specs=[
            pl.BlockSpec((lines, None, res, width), lambda n: (0, plane, 0, 0)),
            pl.BlockSpec(kv.shape, lambda n: (0, 0)),
            pl.BlockSpec((None, lines, res, res), lambda n: (plane, 0, 0, 0)),
            pl.BlockSpec((res, res), lambda n: (0, 0)),
        ],
        out_specs=[
            pl.BlockSpec((lines, res, width), lambda n: (0, 0, 0)),
            pl.BlockSpec((lines, res, LANES), lambda n: (0, 0, 0)),
        ],
        out_shape=[
            jax.ShapeDtypeStruct((lines, res, width), F32),
            jax.ShapeDtypeStruct((lines, res, LANES), F32),
        ],
        scratch_shapes=[pltpu.VMEM((lines, res, 2 * width), BF16)],
        cost_estimate=attention_cost(lines, res, width),
        name=f"near_part_{plane}",
    )(queries, kv, bias, order)


def merge_kernel(far_ref, mean_ref, lse_ref, back_ref, done_ref, out_ref):
    lines, span, width = mean_ref.shape
    res = lines * span
    far = pick(back_ref[...], far_ref[...])
    far_lse = far_sum(far[:, width:].astype(F32))
    near_lse = lse_ref[...].reshape(res, LANES)
    top = jnp.maximum(near_lse, far_lse)
    near_w = jnp.exp(near_lse - top)
    far_w = jnp.exp(far_lse - top)
    scale = 1.0 / (near_w + far_w)
    near_w = near_w * scale
    far_w = far_w * scale
    for h in range(width // HDIM):
        at = pl.ds(h * HDIM, HDIM)
        near = mean_ref[:, :, at].reshape(res, HDIM)
        far_h = far[:, h * HDIM : (h + 1) * HDIM].astype(F32)
        mixed = near * near_w[:, h : h + 1] + far_h * far_w[:, h : h + 1]
        out_ref[:, :, at] = mixed.astype(BF16).reshape(lines, span, HDIM)


def merge_parts(far, mean, lse, back, plane, done):
    lines, planes, res, width = done.shape
    span = res // lines
    return pl.pallas_call(
        merge_kernel,
        grid=(lines,),
        in_specs=[
            pl.BlockSpec((res, width + LANES), lambda c: (c, 0)),
            pl.BlockSpec((lines, span, width), lambda c: (0, c, 0)),
            pl.BlockSpec((lines, span, LANES), lambda c: (0, c, 0)),
            pl.BlockSpec((res, res), lambda c: (0, 0)),
            pl.BlockSpec(memory_space=pl.ANY),
        ],
        out_specs=pl.BlockSpec((lines, None, span, width), lambda c: (0, plane, c, 0)),
        out_shape=jax.ShapeDtypeStruct(done.shape, BF16),
        input_output_aliases={4: 0},
        cost_estimate=pl.CostEstimate(
            flops=2 * lines * res * res * width, bytes_accessed=10 * lines * res * width, transcendentals=0
        ),
        name=f"merge_{plane}",
    )(far, mean, lse, back, done)


def mask_bias(codes, res):
    first_kept = (codes % 2 == 1)[..., None]
    second_kept = (codes >= 2)[..., None]
    kept = jnp.where(jnp.arange(res) < res // 2, first_kept, second_kept)
    return jnp.where(kept, 0.0, -jnp.inf).astype(F32)


def exchange(rows):
    return lax.all_to_all(rows, "seq", split_axis=0, concat_axis=0, tiled=True)


def on_device(count, tokens, queries, key_weight, value_weight, halves):
    scenes, lines, planes, res, depth = tokens.shape
    width = queries.shape[-1]
    tokens = tokens.reshape(lines, planes, res, depth)
    queries = queries.reshape(lines, planes, res, width)
    halves = halves.reshape(lines, planes, 2, 2)
    to_sent = jnp.asarray(home_order(lines, res), BF16)
    to_home = jnp.asarray(home_order(lines, res).T, BF16)
    away = jnp.asarray(away_order(lines, res), BF16)
    from_away = jnp.asarray(away_order(lines, res).T, BF16)

    weight = lax.all_gather(jnp.concatenate([key_weight, value_weight], axis=1), "seq", axis=0, tiled=True)

    dest_half = (np.arange(count) * lines) // (res // 2)
    sent_codes = jnp.where(
        (dest_half == 0)[:, None], halves[:, :, 0, 1].reshape(1, -1), halves[:, :, 1, 1].reshape(1, -1)
    )
    codes = exchange(sent_codes).reshape(res, planes).T
    far_bias = mask_bias(codes, res)
    home_half = jnp.arange(res) // (res // 2)
    near_codes = jnp.where(home_half == 0, halves[:, :, 0:1, 0], halves[:, :, 1:2, 0])
    near_bias = mask_bias(near_codes.transpose(1, 0, 2), res)

    moved = exchange(order_sent(tokens, queries, to_sent))
    far = functools.partial(
        far_attention, moved, bias=far_bias, order=away, back=from_away,
        lead=depth // width, lines=lines, res=res, width=width,
    )
    mean_width = width + LANES
    home_2, sent_2 = project(tokens, weight, to_sent, 2, 2 * width)
    moved_2 = exchange(sent_2)
    home_1, sent_1 = project(tokens, weight, to_sent, 1, 2 * width + mean_width)
    (moved_0,) = project(moved, weight, to_sent, 0, 0)
    sent_1, moved_0 = lax.optimization_barrier((sent_1, moved_0))
    moved_1 = exchange(far(kv=home_2, plane=0, into=sent_1))
    (home_0,) = project(tokens, weight, to_sent, 0, 0)
    mean_2, lse_2 = near_part(queries, moved_0, near_bias, away, 2)
    sent, home_0, mean_2, lse_2 = lax.optimization_barrier((far(kv=moved_2, plane=1), home_0, mean_2, lse_2))
    far_1 = exchange(sent)
    out = near_attention(queries, home_1, near_bias, moved_1, to_home, 0, None)
    sent, out = lax.optimization_barrier((far(kv=moved_1, plane=2), out))
    far_2 = exchange(sent)
    out = near_attention(queries, home_0, near_bias, far_1, to_home, 1, out)
    out = merge_parts(far_2, mean_2, lse_2, to_home, 2, out)
    return out.reshape(scenes, lines, planes, res, width)


def solution(mesh):
    in_specs = (
        P("parts", "seq", None, None, None),
        P("parts", "seq", None, None, None),
        P("seq", None),
        P("seq", None),
        P("parts", "seq", None, None, None),
    )
    return jax.shard_map(
        functools.partial(on_device, mesh.shape["seq"]),
        mesh=mesh,
        in_specs=in_specs,
        out_specs=P("parts", "seq", None, None, None),
        check_vma=False,
    )
```

```python
import functools
import math

import jax
import jax.numpy as jnp
import numpy as np
from jax import lax
from jax.experimental import pallas as pl
from jax.experimental.pallas import tpu as pltpu
from jax.sharding import PartitionSpec as P

HEADS = 12
HDIM = 128
LANES = 128
PLANES = 3
SCALE = 1.0 / math.sqrt(HDIM)
BF16 = jnp.bfloat16
F32 = jnp.float32


def home_order(lines, res):
    span = res // lines
    out = np.zeros((res, res), np.float32)
    for line in range(lines):
        for dest in range(span // lines):
            for pos in range(lines):
                out[(dest * lines + pos) * lines + line, line * span + dest * lines + pos] = 1.0
    return out


def away_order(lines, res):
    span = res // lines
    out = np.zeros((res, res), np.float32)
    for src in range(span // lines):
        for pos in range(lines):
            for line in range(lines):
                out[pos * span + src * lines + line, (src * lines + pos) * lines + line] = 1.0
    return out


def pick(order, rows):
    return jnp.dot(order, rows, preferred_element_type=F32).astype(BF16)


def order_kernel(tokens_ref, queries_ref, order_ref, out_ref):
    lines, res, width = queries_ref.shape
    span = res // lines
    first = pl.program_id(0) < pl.num_programs(0) - PLANES

    def put(ref):
        for i in range(lines):
            rows = ref[:, pl.ds(i * span, span), :].reshape(res, width)
            out_ref[pl.ds(i * res, res), :] = pick(order_ref[...], rows)

    pl.when(first)(lambda: put(tokens_ref))
    pl.when(jnp.logical_not(first))(lambda: put(queries_ref))


def order_sent(tokens, queries, order):
    lines, planes, res, width = queries.shape
    depth = tokens.shape[-1]
    lead = depth // width
    return pl.pallas_call(
        order_kernel,
        grid=(lead + planes,),
        in_specs=[
            pl.BlockSpec((lines, None, res, width), lambda p: (0, 0, 0, jnp.minimum(p, lead - 1))),
            pl.BlockSpec((lines, None, res, width), lambda p: (0, jnp.maximum(p - lead, 0), 0, 0)),
            pl.BlockSpec((res, res), lambda p: (0, 0)),
        ],
        out_specs=pl.BlockSpec((lines * res, width), lambda p: (0, p)),
        out_shape=jax.ShapeDtypeStruct((lines * res, depth + planes * width), BF16),
        cost_estimate=pl.CostEstimate(
            flops=2 * lines * res * (depth + planes * width) * res,
            bytes_accessed=4 * lines * res * (depth + planes * width),
            transcendentals=0,
        ),
        name="order_sent",
    )(tokens, queries, order)


def project_kernel(x_ref, w_ref, order_ref, *out_refs):
    out = jnp.dot(x_ref[...].reshape(-1, x_ref.shape[-1]), w_ref[...], preferred_element_type=F32)
    out = out.astype(BF16)
    tile = w_ref.shape[1]
    home_ref = out_refs[0]
    home_ref[...] = out.reshape(home_ref.shape)
    if len(out_refs) > 1:
        lines, res, _ = x_ref.shape
        span = res // lines
        by_line = out.reshape(lines, res, tile)
        for i in range(lines):
            rows = by_line[:, i * span : (i + 1) * span].reshape(res, tile)
            out_refs[1][pl.ds(i * res, res), :] = pick(order_ref[...], rows)


def project(tokens, weight, order, plane, sent_width):
    depth, width = weight.shape
    tile = 512
    if tokens.ndim == 4:
        lines, planes, res, _ = tokens.shape
        x_spec = pl.BlockSpec((lines, None, res, depth), lambda n: (0, plane, 0, 0))
        rows = lines * res
        out_specs = [pl.BlockSpec((lines, res, tile), lambda n: (0, 0, n))]
        out_shape = [jax.ShapeDtypeStruct((lines, res, width), BF16)]
    else:
        rows = tokens.shape[0]
        x_spec = pl.BlockSpec((rows, depth), lambda n: (0, 0))
        out_specs = [pl.BlockSpec((rows, tile), lambda n: (0, n))]
        out_shape = [jax.ShapeDtypeStruct((rows, width), BF16)]
    if sent_width:
        out_specs.append(pl.BlockSpec((rows, tile), lambda n: (0, n)))
        out_shape.append(jax.ShapeDtypeStruct((rows, sent_width), BF16))
    return pl.pallas_call(
        project_kernel,
        grid=(width // tile,),
        in_specs=[
            x_spec,
            pl.BlockSpec((depth, tile), lambda n: (0, n)),
            pl.BlockSpec(order.shape, lambda n: (0, 0)),
        ],
        out_specs=out_specs,
        out_shape=out_shape,
        cost_estimate=pl.CostEstimate(
            flops=2 * rows * depth * width,
            bytes_accessed=2 * (rows * (depth + 2 * width) + depth * width),
            transcendentals=0,
        ),
        name=f"project_{plane}",
    )(tokens, weight, order)


def to_away(src_ref, order_ref, dst_ref):
    lines, res, width = dst_ref.shape
    span = res // lines
    for c in range(lines):
        rows = pick(order_ref[...], src_ref[pl.ds(c * res, res), :])
        for pos in range(lines):
            dst_ref[pos, pl.ds(c * span, span), :] = rows[pos * span : (pos + 1) * span]


def attend(q, k, v, bias):
    scores = lax.dot_general(q, k, (((1,), (1,)), ((), ())), preferred_element_type=F32)
    scores = scores * SCALE + bias
    peak = jnp.max(scores, axis=1, keepdims=True)
    weights = jnp.exp(scores - peak)
    total = jnp.sum(weights, axis=1, keepdims=True)
    out = jnp.dot(weights.astype(BF16), v, preferred_element_type=F32)
    return out, peak, total


def far_kernel(moved_kv, column, q_ref, kv_ref, bias_ref, order_ref, back_ref, *rest):
    out_ref, q_s, kv_s, mean_s, sent_s, sem = rest[-6:]
    lines, res, width = q_s.shape
    span = res // lines
    heads = width // HDIM
    to_away(q_ref, order_ref, q_s)
    if moved_kv:
        to_away(kv_ref, order_ref, kv_s)
    else:
        kv_s = kv_ref
    lane = lax.broadcasted_iota(jnp.int32, (res, LANES), 1)

    def step(i, carry):
        lse = jnp.zeros((res, LANES), F32)
        for h in range(heads):
            at = pl.ds(h * HDIM, HDIM)
            out, peak, total = attend(
                q_s[i, :, at], kv_s[i, :, at], kv_s[i, :, pl.ds(width + h * HDIM, HDIM)], bias_ref[...]
            )
            mean_s[i, :, at] = (out * (1.0 / total)).astype(BF16)
            lse = jnp.where(lane == h, peak + jnp.log(total), lse)
        high = lse.astype(BF16).astype(F32)
        mid = (lse - high).astype(BF16).astype(F32)
        low = (lse - high - mid).astype(BF16).astype(F32)
        parts = high + pltpu.roll(mid, 16, 1) + pltpu.roll(low, 32, 1)
        mean_s[i, :, pl.ds(width, LANES)] = parts.astype(BF16)
        return carry

    lax.fori_loop(0, lines, step, 0)
    for c in range(lines):
        rows = jnp.concatenate([mean_s[pos, pl.ds(c * span, span), :] for pos in range(lines)], axis=0)
        sent_s[pl.ds(c * res, res), :] = pick(back_ref[...], rows)
    copy = pltpu.make_async_copy(sent_s, out_ref.at[:, pl.ds(column, width + LANES)], sem)
    copy.start()
    copy.wait()


VMEM_SPEC = pl.BlockSpec(memory_space=pltpu.VMEM)


def attention_cost(lines, res, width):
    return pl.CostEstimate(
        flops=4 * lines * res * res * width,
        bytes_accessed=2 * lines * res * width * 5,
        transcendentals=lines * res * res * (width // HDIM),
    )


def far_attention(moved_q, kv, bias, order, back, plane, lead, lines, res, width, into=None):
    moved_kv = kv.ndim == 2
    kv_shape = (lines, res, 2 * width) if moved_kv else (1, 16, LANES)
    kv_block = kv.shape[:-1] + (2 * width,)
    column = 0 if into is None else into.shape[1] - width - LANES
    shape = (lines * res, column + width + LANES)
    in_specs = [
        pl.BlockSpec((lines * res, width), lambda n: (0, lead + plane)),
        pl.BlockSpec(kv_block, lambda n: (0,) * kv.ndim),
        pl.BlockSpec((None, res, res), lambda n: (plane, 0, 0)),
        pl.BlockSpec((res, res), lambda n: (0, 0)),
        pl.BlockSpec((res, res), lambda n: (0, 0)),
    ]
    args = (moved_q, kv, bias, order, back)
    if into is not None:
        in_specs.append(pl.BlockSpec(memory_space=pl.ANY))
        args = args + (into,)
    return pl.pallas_call(
        functools.partial(far_kernel, moved_kv, column),
        grid=(1,),
        in_specs=in_specs,
        out_specs=pl.BlockSpec(memory_space=pl.ANY),
        out_shape=jax.ShapeDtypeStruct(shape, BF16),
        scratch_shapes=[
            pltpu.VMEM((lines, res, width), BF16),
            pltpu.VMEM(kv_shape, BF16),
            pltpu.VMEM((lines, res, width + LANES), BF16),
            pltpu.VMEM((lines * res, width + LANES), BF16),
            pltpu.SemaphoreType.DMA,
        ],
        input_output_aliases={} if into is None else {5: 0},
        cost_estimate=attention_cost(lines, res, width),
        name=f"far_{plane}",
    )(*args)


def far_sum(parts):
    return parts + pltpu.roll(parts, LANES - 16, 1) + pltpu.roll(parts, LANES - 32, 1)


def near_kernel(column, q_ref, kv_ref, bias_ref, far_ref, back_ref, *rest):
    out_ref, far_s = rest[-2:]
    lines, res, width = q_ref.shape
    span = res // lines
    heads = width // HDIM
    for c in range(lines):
        rows = pick(back_ref[...], far_ref[pl.ds(c * res, res), pl.ds(column, width + LANES)])
        for line in range(lines):
            far_s[line, pl.ds(c * span, span), :] = rows[line * span : (line + 1) * span]

    def step(i, carry):
        lse = far_sum(far_s[i, :, pl.ds(width, LANES)].astype(F32))
        for h in range(heads):
            at = pl.ds(h * HDIM, HDIM)
            out, peak, total = attend(
                q_ref[i, :, at], kv_ref[i, :, at], kv_ref[i, :, pl.ds(width + h * HDIM, HDIM)], bias_ref[i]
            )
            far_lse = lse[:, h : h + 1]
            top = jnp.maximum(peak, far_lse)
            near_w = jnp.exp(peak - top)
            far_w = jnp.exp(far_lse - top)
            scale = 1.0 / (total * near_w + far_w)
            mixed = out * (near_w * scale) + far_s[i, :, at].astype(F32) * (far_w * scale)
            out_ref[i, :, at] = mixed.astype(BF16)
        return carry

    lax.fori_loop(0, lines, step, 0)


def near_attention(queries, kv, bias, far, back, plane, done):
    lines, planes, res, width = queries.shape
    in_specs = [
        pl.BlockSpec((lines, None, res, width), lambda n: (0, plane, 0, 0)),
        pl.BlockSpec(kv.shape, lambda n: (0,) * kv.ndim),
        pl.BlockSpec((None, lines, res, res), lambda n: (plane, 0, 0, 0)),
        pl.BlockSpec(far.shape, lambda n: (0, 0)),
        pl.BlockSpec((res, res), lambda n: (0, 0)),
    ]
    args = (queries, kv, bias, far, back)
    if done is not None:
        in_specs.append(pl.BlockSpec(memory_space=pl.ANY))
        args = args + (done,)
    return pl.pallas_call(
        functools.partial(near_kernel, far.shape[1] - width - LANES),
        grid=(1,),
        in_specs=in_specs,
        out_specs=pl.BlockSpec((lines, None, res, width), lambda n: (0, plane, 0, 0)),
        out_shape=jax.ShapeDtypeStruct(queries.shape, BF16),
        scratch_shapes=[pltpu.VMEM((lines, res, width + LANES), BF16)],
        input_output_aliases={} if done is None else {5: 0},
        cost_estimate=attention_cost(lines, res, width),
        name=f"near_{plane}",
    )(*args)


def part_kernel(q_ref, kv_ref, bias_ref, order_ref, mean_ref, lse_ref, kv_s):
    lines, res, width = q_ref.shape
    heads = width // HDIM
    to_away(kv_ref, order_ref, kv_s)
    lane = lax.broadcasted_iota(jnp.int32, (res, LANES), 1)

    def step(i, carry):
        lse = jnp.zeros((res, LANES), F32)
        for h in range(heads):
            at = pl.ds(h * HDIM, HDIM)
            out, peak, total = attend(
                q_ref[i, :, at], kv_s[i, :, at], kv_s[i, :, pl.ds(width + h * HDIM, HDIM)], bias_ref[i]
            )
            mean_ref[i, :, at] = out * (1.0 / total)
            lse = jnp.where(lane == h, peak + jnp.log(total), lse)
        lse_ref[i] = lse
        return carry

    lax.fori_loop(0, lines, step, 0)


def near_part(queries, kv, bias, order, plane):
    lines, planes, res, width = queries.shape
    return pl.pallas_call(
        part_kernel,
        grid=(1,),
        in_specs=[
            pl.BlockSpec((lines, None, res, width), lambda n: (0, plane, 0, 0)),
            pl.BlockSpec(kv.shape, lambda n: (0, 0)),
            pl.BlockSpec((None, lines, res, res), lambda n: (plane, 0, 0, 0)),
            pl.BlockSpec((res, res), lambda n: (0, 0)),
        ],
        out_specs=[
            pl.BlockSpec((lines, res, width), lambda n: (0, 0, 0)),
            pl.BlockSpec((lines, res, LANES), lambda n: (0, 0, 0)),
        ],
        out_shape=[
            jax.ShapeDtypeStruct((lines, res, width), F32),
            jax.ShapeDtypeStruct((lines, res, LANES), F32),
        ],
        scratch_shapes=[pltpu.VMEM((lines, res, 2 * width), BF16)],
        cost_estimate=attention_cost(lines, res, width),
        name=f"near_part_{plane}",
    )(queries, kv, bias, order)


def merge_kernel(far_ref, mean_ref, lse_ref, back_ref, done_ref, out_ref):
    lines, span, width = mean_ref.shape
    res = lines * span
    far = pick(back_ref[...], far_ref[...])
    far_lse = far_sum(far[:, width:].astype(F32))
    near_lse = lse_ref[...].reshape(res, LANES)
    top = jnp.maximum(near_lse, far_lse)
    near_w = jnp.exp(near_lse - top)
    far_w = jnp.exp(far_lse - top)
    scale = 1.0 / (near_w + far_w)
    near_w = near_w * scale
    far_w = far_w * scale
    for h in range(width // HDIM):
        at = pl.ds(h * HDIM, HDIM)
        near = mean_ref[:, :, at].reshape(res, HDIM)
        far_h = far[:, h * HDIM : (h + 1) * HDIM].astype(F32)
        mixed = near * near_w[:, h : h + 1] + far_h * far_w[:, h : h + 1]
        out_ref[:, :, at] = mixed.astype(BF16).reshape(lines, span, HDIM)


def merge_parts(far, mean, lse, back, plane, done):
    lines, planes, res, width = done.shape
    span = res // lines
    return pl.pallas_call(
        merge_kernel,
        grid=(lines,),
        in_specs=[
            pl.BlockSpec((res, width + LANES), lambda c: (c, 0)),
            pl.BlockSpec((lines, span, width), lambda c: (0, c, 0)),
            pl.BlockSpec((lines, span, LANES), lambda c: (0, c, 0)),
            pl.BlockSpec((res, res), lambda c: (0, 0)),
            pl.BlockSpec(memory_space=pl.ANY),
        ],
        out_specs=pl.BlockSpec((lines, None, span, width), lambda c: (0, plane, c, 0)),
        out_shape=jax.ShapeDtypeStruct(done.shape, BF16),
        input_output_aliases={4: 0},
        cost_estimate=pl.CostEstimate(
            flops=2 * lines * res * res * width, bytes_accessed=10 * lines * res * width, transcendentals=0
        ),
        name=f"merge_{plane}",
    )(far, mean, lse, back, done)


def mask_bias(codes, res):
    first_kept = (codes % 2 == 1)[..., None]
    second_kept = (codes >= 2)[..., None]
    kept = jnp.where(jnp.arange(res) < res // 2, first_kept, second_kept)
    return jnp.where(kept, 0.0, -jnp.inf).astype(F32)


def exchange(rows):
    return lax.all_to_all(rows, "seq", split_axis=0, concat_axis=0, tiled=True)


def gather_weight(shard, count, sent, codes):
    outer = 1
    while outer * outer < count // 2:
        outer *= 2
    inner = count // outer
    across = [[o * inner + i for o in range(outer)] for i in range(inner)]
    within = [[o * inner + i for i in range(inner)] for o in range(outer)]
    blocks = lax.all_gather(shard[None], "seq", axis=0, tiled=True, axis_index_groups=across)
    blocks, sent, codes = lax.optimization_barrier((blocks, sent, codes))
    blocks = lax.all_gather(blocks, "seq", axis=1, tiled=True, axis_index_groups=within)
    return blocks.reshape(-1, shard.shape[-1]), sent, codes


def on_device(count, tokens, queries, key_weight, value_weight, halves):
    scenes, lines, planes, res, depth = tokens.shape
    width = queries.shape[-1]
    tokens = tokens.reshape(lines, planes, res, depth)
    queries = queries.reshape(lines, planes, res, width)
    halves = halves.reshape(lines, planes, 2, 2)
    to_sent = jnp.asarray(home_order(lines, res), BF16)
    to_home = jnp.asarray(home_order(lines, res).T, BF16)
    away = jnp.asarray(away_order(lines, res), BF16)
    from_away = jnp.asarray(away_order(lines, res).T, BF16)

    dest_half = (np.arange(count) * lines) // (res // 2)
    sent_codes = jnp.where(
        (dest_half == 0)[:, None], halves[:, :, 0, 1].reshape(1, -1), halves[:, :, 1, 1].reshape(1, -1)
    )
    codes = exchange(sent_codes)
    sent = order_sent(tokens, queries, to_sent)
    weight, sent, codes = gather_weight(jnp.concatenate([key_weight, value_weight], axis=1), count, sent, codes)
    codes = codes.reshape(res, planes).T
    far_bias = mask_bias(codes, res)
    home_half = jnp.arange(res) // (res // 2)
    near_codes = jnp.where(home_half == 0, halves[:, :, 0:1, 0], halves[:, :, 1:2, 0])
    near_bias = mask_bias(near_codes.transpose(1, 0, 2), res)

    moved = exchange(sent)
    far = functools.partial(
        far_attention, moved, bias=far_bias, order=away, back=from_away,
        lead=depth // width, lines=lines, res=res, width=width,
    )
    mean_width = width + LANES
    home_2, sent_2 = project(tokens, weight, to_sent, 2, 2 * width)
    moved_2 = exchange(sent_2)
    home_1, sent_1 = project(tokens, weight, to_sent, 1, 2 * width + mean_width)
    (moved_0,) = project(moved, weight, to_sent, 0, 0)
    sent_1, moved_0 = lax.optimization_barrier((sent_1, moved_0))
    moved_1 = exchange(far(kv=home_2, plane=0, into=sent_1))
    (home_0,) = project(tokens, weight, to_sent, 0, 0)
    mean_2, lse_2 = near_part(queries, moved_0, near_bias, away, 2)
    sent, home_0, mean_2, lse_2 = lax.optimization_barrier((far(kv=moved_2, plane=1), home_0, mean_2, lse_2))
    far_1 = exchange(sent)
    out = near_attention(queries, home_1, near_bias, moved_1, to_home, 0, None)
    sent, out = lax.optimization_barrier((far(kv=moved_1, plane=2), out))
    far_2 = exchange(sent)
    out = near_attention(queries, home_0, near_bias, far_1, to_home, 1, out)
    out = merge_parts(far_2, mean_2, lse_2, to_home, 2, out)
    return out.reshape(scenes, lines, planes, res, width)


def solution(mesh):
    in_specs = (
        P("parts", "seq", None, None, None),
        P("parts", "seq", None, None, None),
        P("seq", None),
        P("seq", None),
        P("parts", "seq", None, None, None),
    )
    return jax.shard_map(
        functools.partial(on_device, mesh.shape["seq"]),
        mesh=mesh,
        in_specs=in_specs,
        out_specs=P("parts", "seq", None, None, None),
        check_vma=False,
    )
```

```python
import functools
import math

import jax
import jax.numpy as jnp
import numpy as np
from jax import lax
from jax.experimental import pallas as pl
from jax.experimental.pallas import tpu as pltpu
from jax.sharding import PartitionSpec as P

HEADS = 12
HDIM = 128
LANES = 128
SCALE = 1.0 / math.sqrt(HDIM)
BF16 = jnp.bfloat16
F32 = jnp.float32


def home_order(lines, res):
    span = res // lines
    out = np.zeros((res, res), np.float32)
    for line in range(lines):
        for dest in range(span // lines):
            for pos in range(lines):
                out[(dest * lines + pos) * lines + line, line * span + dest * lines + pos] = 1.0
    return out


def away_order(lines, res):
    span = res // lines
    out = np.zeros((res, res), np.float32)
    for src in range(span // lines):
        for pos in range(lines):
            for line in range(lines):
                out[pos * span + src * lines + line, (src * lines + pos) * lines + line] = 1.0
    return out


def pick(order, rows):
    return jnp.dot(order, rows, preferred_element_type=F32).astype(BF16)


def order_kernel(lead, tokens_ref, queries_ref, order_ref, out_ref):
    lines, res, width = queries_ref.shape
    span = res // lines
    first = pl.program_id(0) < lead

    def put(ref):
        for i in range(lines):
            rows = ref[:, pl.ds(i * span, span), :].reshape(res, width)
            out_ref[pl.ds(i * res, res), :] = pick(order_ref[...], rows)

    pl.when(first)(lambda: put(tokens_ref))
    pl.when(jnp.logical_not(first))(lambda: put(queries_ref))


def order_sent(tokens, queries, order, token_planes):
    lines, planes, res, width = queries.shape
    depth = tokens.shape[-1]
    parts = depth // width
    lead = token_planes * parts
    columns = (lead + planes) * width

    def token_block(p):
        p = jnp.minimum(p, lead - 1)
        return 0, p // parts, 0, p % parts

    return pl.pallas_call(
        functools.partial(order_kernel, lead),
        grid=(lead + planes,),
        in_specs=[
            pl.BlockSpec((lines, None, res, width), token_block),
            pl.BlockSpec((lines, None, res, width), lambda p: (0, jnp.maximum(p - lead, 0), 0, 0)),
            pl.BlockSpec((res, res), lambda p: (0, 0)),
        ],
        out_specs=pl.BlockSpec((lines * res, width), lambda p: (0, p)),
        out_shape=jax.ShapeDtypeStruct((lines * res, columns), BF16),
        cost_estimate=pl.CostEstimate(
            flops=2 * lines * res * columns * res, bytes_accessed=4 * lines * res * columns, transcendentals=0
        ),
        name="order_sent",
    )(tokens, queries, order)


def project_kernel(x_ref, w_ref, order_ref, *out_refs):
    out = jnp.dot(x_ref[...].reshape(-1, x_ref.shape[-1]), w_ref[...], preferred_element_type=F32)
    out = out.astype(BF16)
    tile = w_ref.shape[1]
    home_ref = out_refs[0]
    home_ref[...] = out.reshape(home_ref.shape)
    if len(out_refs) > 1:
        lines, res, _ = x_ref.shape
        span = res // lines
        by_line = out.reshape(lines, res, tile)
        for i in range(lines):
            rows = by_line[:, i * span : (i + 1) * span].reshape(res, tile)
            out_refs[1][pl.ds(i * res, res), :] = pick(order_ref[...], rows)


def project(tokens, weight, order, plane, sent_width):
    depth, width = weight.shape
    tile = 512
    if tokens.ndim == 4:
        lines, planes, res, _ = tokens.shape
        x_spec = pl.BlockSpec((lines, None, res, depth), lambda n: (0, plane, 0, 0))
        rows = lines * res
        out_specs = [pl.BlockSpec((lines, res, tile), lambda n: (0, 0, n))]
        out_shape = [jax.ShapeDtypeStruct((lines, res, width), BF16)]
    else:
        rows = tokens.shape[0]
        x_spec = pl.BlockSpec((rows, depth), lambda n: (0, plane))
        out_specs = [pl.BlockSpec((rows, tile), lambda n: (0, n))]
        out_shape = [jax.ShapeDtypeStruct((rows, width), BF16)]
    if sent_width:
        out_specs.append(pl.BlockSpec((rows, tile), lambda n: (0, n)))
        out_shape.append(jax.ShapeDtypeStruct((rows, sent_width), BF16))
    return pl.pallas_call(
        project_kernel,
        grid=(width // tile,),
        in_specs=[
            x_spec,
            pl.BlockSpec((depth, tile), lambda n: (0, n)),
            pl.BlockSpec(order.shape, lambda n: (0, 0)),
        ],
        out_specs=out_specs,
        out_shape=out_shape,
        cost_estimate=pl.CostEstimate(
            flops=2 * rows * depth * width,
            bytes_accessed=2 * (rows * (depth + 2 * width) + depth * width),
            transcendentals=0,
        ),
        name=f"project_{plane}",
    )(tokens, weight, order)


def to_away(src_ref, order_ref, dst_ref):
    lines, res, width = dst_ref.shape
    span = res // lines
    for c in range(lines):
        rows = pick(order_ref[...], src_ref[pl.ds(c * res, res), :])
        for pos in range(lines):
            dst_ref[pos, pl.ds(c * span, span), :] = rows[pos * span : (pos + 1) * span]


def attend(q, k, v, bias):
    scores = lax.dot_general(q, k, (((1,), (1,)), ((), ())), preferred_element_type=F32)
    scores = scores * SCALE + bias
    peak = jnp.max(scores, axis=1, keepdims=True)
    weights = jnp.exp(scores - peak)
    total = jnp.sum(weights, axis=1, keepdims=True)
    out = jnp.dot(weights.astype(BF16), v, preferred_element_type=F32)
    return out, peak, total


def far_kernel(moved_kv, column, q_ref, kv_ref, bias_ref, order_ref, back_ref, *rest):
    out_ref, q_s, kv_s, mean_s, sent_s, sem = rest[-6:]
    lines, res, width = q_s.shape
    span = res // lines
    heads = width // HDIM
    to_away(q_ref, order_ref, q_s)
    if moved_kv:
        to_away(kv_ref, order_ref, kv_s)
    else:
        kv_s = kv_ref
    lane = lax.broadcasted_iota(jnp.int32, (res, LANES), 1)

    def step(i, carry):
        lse = jnp.zeros((res, LANES), F32)
        for h in range(heads):
            at = pl.ds(h * HDIM, HDIM)
            out, peak, total = attend(
                q_s[i, :, at], kv_s[i, :, at], kv_s[i, :, pl.ds(width + h * HDIM, HDIM)], bias_ref[...]
            )
            mean_s[i, :, at] = (out * (1.0 / total)).astype(BF16)
            lse = jnp.where(lane == h, peak + jnp.log(total), lse)
        high = lse.astype(BF16).astype(F32)
        mid = (lse - high).astype(BF16).astype(F32)
        low = (lse - high - mid).astype(BF16).astype(F32)
        parts = high + pltpu.roll(mid, 16, 1) + pltpu.roll(low, 32, 1)
        mean_s[i, :, pl.ds(width, LANES)] = parts.astype(BF16)
        return carry

    lax.fori_loop(0, lines, step, 0)
    for c in range(lines):
        rows = jnp.concatenate([mean_s[pos, pl.ds(c * span, span), :] for pos in range(lines)], axis=0)
        sent_s[pl.ds(c * res, res), :] = pick(back_ref[...], rows)
    copy = pltpu.make_async_copy(sent_s, out_ref.at[:, pl.ds(column, width + LANES)], sem)
    copy.start()
    copy.wait()


VMEM_SPEC = pl.BlockSpec(memory_space=pltpu.VMEM)


def attention_cost(lines, res, width):
    return pl.CostEstimate(
        flops=4 * lines * res * res * width,
        bytes_accessed=2 * lines * res * width * 5,
        transcendentals=lines * res * res * (width // HDIM),
    )


def far_attention(moved_q, kv, bias, order, back, plane, lead, lines, res, width, slot=0, slots=1, into=None):
    moved_kv = kv.ndim == 2
    kv_shape = (lines, res, 2 * width) if moved_kv else (1, 16, LANES)
    kv_block = kv.shape[:-1] + (2 * width,)
    column = slot * (width + LANES)
    shape = (lines * res, slots * (width + LANES))
    in_specs = [
        pl.BlockSpec((lines * res, width), lambda n: (0, lead + plane)),
        pl.BlockSpec(kv_block, lambda n: (0,) * kv.ndim),
        pl.BlockSpec((None, res, res), lambda n: (plane, 0, 0)),
        pl.BlockSpec((res, res), lambda n: (0, 0)),
        pl.BlockSpec((res, res), lambda n: (0, 0)),
    ]
    args = (moved_q, kv, bias, order, back)
    if into is not None:
        in_specs.append(pl.BlockSpec(memory_space=pl.ANY))
        args = args + (into,)
    return pl.pallas_call(
        functools.partial(far_kernel, moved_kv, column),
        grid=(1,),
        in_specs=in_specs,
        out_specs=pl.BlockSpec(memory_space=pl.ANY),
        out_shape=jax.ShapeDtypeStruct(shape, BF16),
        scratch_shapes=[
            pltpu.VMEM((lines, res, width), BF16),
            pltpu.VMEM(kv_shape, BF16),
            pltpu.VMEM((lines, res, width + LANES), BF16),
            pltpu.VMEM((lines * res, width + LANES), BF16),
            pltpu.SemaphoreType.DMA,
        ],
        input_output_aliases={} if into is None else {5: 0},
        cost_estimate=attention_cost(lines, res, width),
        name=f"far_{plane}",
    )(*args)


def far_sum(parts):
    return parts + pltpu.roll(parts, LANES - 16, 1) + pltpu.roll(parts, LANES - 32, 1)


def part_kernel(q_ref, kv_ref, bias_ref, order_ref, mean_ref, lse_ref, kv_s):
    lines, res, width = q_ref.shape
    heads = width // HDIM
    if len(kv_ref.shape) == 2:
        to_away(kv_ref, order_ref, kv_s)
    else:
        kv_s = kv_ref
    lane = lax.broadcasted_iota(jnp.int32, (res, LANES), 1)

    def step(i, carry):
        lse = jnp.zeros((res, LANES), F32)
        for h in range(heads):
            at = pl.ds(h * HDIM, HDIM)
            out, peak, total = attend(
                q_ref[i, :, at], kv_s[i, :, at], kv_s[i, :, pl.ds(width + h * HDIM, HDIM)], bias_ref[i]
            )
            mean_ref[i, :, at] = out * (1.0 / total)
            lse = jnp.where(lane == h, peak + jnp.log(total), lse)
        lse_ref[i] = lse
        return carry

    lax.fori_loop(0, lines, step, 0)


def near_part(queries, kv, bias, order, plane):
    lines, planes, res, width = queries.shape
    return pl.pallas_call(
        part_kernel,
        grid=(1,),
        in_specs=[
            pl.BlockSpec((lines, None, res, width), lambda n: (0, plane, 0, 0)),
            pl.BlockSpec(kv.shape, lambda n: (0,) * kv.ndim),
            pl.BlockSpec((None, lines, res, res), lambda n: (plane, 0, 0, 0)),
            pl.BlockSpec((res, res), lambda n: (0, 0)),
        ],
        out_specs=[
            pl.BlockSpec((lines, res, width), lambda n: (0, 0, 0)),
            pl.BlockSpec((lines, res, LANES), lambda n: (0, 0, 0)),
        ],
        out_shape=[
            jax.ShapeDtypeStruct((lines, res, width), F32),
            jax.ShapeDtypeStruct((lines, res, LANES), F32),
        ],
        scratch_shapes=[pltpu.VMEM((lines, res, 2 * width) if kv.ndim == 2 else (1, 16, LANES), BF16)],
        cost_estimate=attention_cost(lines, res, width),
        name=f"near_part_{plane}",
    )(queries, kv, bias, order)


def merge_kernel(far_ref, mean_ref, lse_ref, back_ref, *rest):
    out_ref = rest[-1]
    lines, span, width = mean_ref.shape
    res = lines * span
    far = pick(back_ref[...], far_ref[...])
    far_lse = far_sum(far[:, width:].astype(F32))
    near_lse = lse_ref[...].reshape(res, LANES)
    top = jnp.maximum(near_lse, far_lse)
    near_w = jnp.exp(near_lse - top)
    far_w = jnp.exp(far_lse - top)
    scale = 1.0 / (near_w + far_w)
    near_w = near_w * scale
    far_w = far_w * scale
    for h in range(width // HDIM):
        at = pl.ds(h * HDIM, HDIM)
        near = mean_ref[:, :, at].reshape(res, HDIM)
        far_h = far[:, h * HDIM : (h + 1) * HDIM].astype(F32)
        mixed = near * near_w[:, h : h + 1] + far_h * far_w[:, h : h + 1]
        out_ref[:, :, at] = mixed.astype(BF16).reshape(lines, span, HDIM)


def merge_parts(far, slot, near, back, plane, planes, done):
    mean, lse = near
    lines, res, width = mean.shape
    span = res // lines
    in_specs = [
        pl.BlockSpec((res, width + LANES), lambda c: (c, slot)),
        pl.BlockSpec((lines, span, width), lambda c: (0, c, 0)),
        pl.BlockSpec((lines, span, LANES), lambda c: (0, c, 0)),
        pl.BlockSpec((res, res), lambda c: (0, 0)),
    ]
    args = (far, mean, lse, back)
    if done is not None:
        in_specs.append(pl.BlockSpec(memory_space=pl.ANY))
        args = args + (done,)
    return pl.pallas_call(
        merge_kernel,
        grid=(lines,),
        in_specs=in_specs,
        out_specs=pl.BlockSpec((lines, None, span, width), lambda c: (0, plane, c, 0)),
        out_shape=jax.ShapeDtypeStruct((lines, planes, res, width), BF16),
        input_output_aliases={} if done is None else {4: 0},
        cost_estimate=pl.CostEstimate(
            flops=2 * lines * res * res * width, bytes_accessed=10 * lines * res * width, transcendentals=0
        ),
        name=f"merge_{plane}",
    )(*args)


def mask_bias(codes, res):
    first_kept = (codes % 2 == 1)[..., None]
    second_kept = (codes >= 2)[..., None]
    kept = jnp.where(jnp.arange(res) < res // 2, first_kept, second_kept)
    return jnp.where(kept, 0.0, -jnp.inf).astype(F32)


def exchange(rows):
    return lax.all_to_all(rows, "seq", split_axis=0, concat_axis=0, tiled=True)


def gather_weight(shard, count, sent, codes):
    outer = 1
    while outer * outer < count // 2:
        outer *= 2
    inner = count // outer
    across = [[o * inner + i for o in range(outer)] for i in range(inner)]
    within = [[o * inner + i for i in range(inner)] for o in range(outer)]
    blocks = lax.all_gather(shard[None], "seq", axis=0, tiled=True, axis_index_groups=across)
    blocks, sent, codes = lax.optimization_barrier((blocks, sent, codes))
    blocks = lax.all_gather(blocks, "seq", axis=1, tiled=True, axis_index_groups=within)
    return blocks.reshape(-1, shard.shape[-1]), sent, codes


def on_device(count, tokens, queries, key_weight, value_weight, halves):
    scenes, lines, planes, res, depth = tokens.shape
    width = queries.shape[-1]
    tokens = tokens.reshape(lines, planes, res, depth)
    queries = queries.reshape(lines, planes, res, width)
    halves = halves.reshape(lines, planes, 2, 2)
    to_sent = jnp.asarray(home_order(lines, res), BF16)
    to_home = jnp.asarray(home_order(lines, res).T, BF16)
    away = jnp.asarray(away_order(lines, res), BF16)
    from_away = jnp.asarray(away_order(lines, res).T, BF16)

    dest_half = (np.arange(count) * lines) // (res // 2)
    sent_codes = jnp.where(
        (dest_half == 0)[:, None], halves[:, :, 0, 1].reshape(1, -1), halves[:, :, 1, 1].reshape(1, -1)
    )
    codes = exchange(sent_codes)
    token_planes = 2
    sent = order_sent(tokens, queries, to_sent, token_planes)
    weight, sent, codes = gather_weight(jnp.concatenate([key_weight, value_weight], axis=1), count, sent, codes)
    codes = codes.reshape(res, planes).T
    far_bias = mask_bias(codes, res)
    home_half = jnp.arange(res) // (res // 2)
    near_codes = jnp.where(home_half == 0, halves[:, :, 0:1, 0], halves[:, :, 1:2, 0])
    near_bias = mask_bias(near_codes.transpose(1, 0, 2), res)

    moved = exchange(sent)
    far = functools.partial(
        far_attention, moved, bias=far_bias, order=away, back=from_away,
        lead=token_planes * depth // width, lines=lines, res=res, width=width,
    )
    near = functools.partial(near_part, queries, bias=near_bias, order=away)
    merge = functools.partial(merge_parts, back=to_home, planes=planes)
    home_2, sent_2 = project(tokens, weight, to_sent, 2, 2 * width)
    (home_0,) = project(tokens, weight, to_sent, 0, 0)
    sent_2, home_0 = lax.optimization_barrier((sent_2, home_0))
    moved_2 = exchange(sent_2)
    (moved_1,) = project(moved, weight, to_sent, 1, 0)
    (home_1,) = project(tokens, weight, to_sent, 1, 0)
    sent = far(kv=home_2, plane=0, slots=2)
    sent = far(kv=moved_1, plane=2, slot=1, slots=2, into=sent)
    sent, home_1 = lax.optimization_barrier((sent, home_1))
    far_02 = exchange(sent)
    (moved_0,) = project(moved, weight, to_sent, 0, 0)
    near_2 = near(kv=moved_0, plane=2)
    near_1 = near(kv=home_0, plane=1)
    sent, near_1, near_2 = lax.optimization_barrier((far(kv=moved_2, plane=1), near_1, near_2))
    far_1 = exchange(sent)
    near_0 = near(kv=home_1, plane=0)
    out = merge(far_02, 0, near_0, plane=0, done=None)
    out = merge(far_02, 1, near_2, plane=2, done=out)
    out = merge(far_1, 0, near_1, plane=1, done=out)
    return out.reshape(scenes, lines, planes, res, width)


def solution(mesh):
    in_specs = (
        P("parts", "seq", None, None, None),
        P("parts", "seq", None, None, None),
        P("seq", None),
        P("seq", None),
        P("parts", "seq", None, None, None),
    )
    return jax.shard_map(
        functools.partial(on_device, mesh.shape["seq"]),
        mesh=mesh,
        in_specs=in_specs,
        out_specs=P("parts", "seq", None, None, None),
        check_vma=False,
    )
```

```python
import functools
import math

import jax
import jax.numpy as jnp
import numpy as np
from jax import lax
from jax.experimental import pallas as pl
from jax.experimental.pallas import tpu as pltpu
from jax.sharding import PartitionSpec as P

HEADS = 12
HDIM = 128
LANES = 128
SCALE = 1.0 / math.sqrt(HDIM)
BF16 = jnp.bfloat16
F32 = jnp.float32


def home_order(lines, res):
    span = res // lines
    out = np.zeros((res, res), np.float32)
    for line in range(lines):
        for dest in range(span // lines):
            for pos in range(lines):
                out[(dest * lines + pos) * lines + line, line * span + dest * lines + pos] = 1.0
    return out


def away_order(lines, res):
    span = res // lines
    out = np.zeros((res, res), np.float32)
    for src in range(span // lines):
        for pos in range(lines):
            for line in range(lines):
                out[pos * span + src * lines + line, (src * lines + pos) * lines + line] = 1.0
    return out


def pick(order, rows):
    return jnp.dot(order, rows, preferred_element_type=F32).astype(BF16)


def order_kernel(lead, tokens_ref, queries_ref, order_ref, out_ref):
    lines, res, width = queries_ref.shape
    span = res // lines
    first = pl.program_id(0) < lead

    def put(ref):
        for i in range(lines):
            rows = ref[:, pl.ds(i * span, span), :].reshape(res, width)
            out_ref[pl.ds(i * res, res), :] = pick(order_ref[...], rows)

    pl.when(first)(lambda: put(tokens_ref))
    pl.when(jnp.logical_not(first))(lambda: put(queries_ref))


def order_sent(tokens, queries, order, token_planes):
    lines, planes, res, width = queries.shape
    depth = tokens.shape[-1]
    parts = depth // width
    lead = token_planes * parts
    columns = (lead + planes) * width

    def token_block(p):
        p = jnp.minimum(p, lead - 1)
        return 0, p // parts, 0, p % parts

    return pl.pallas_call(
        functools.partial(order_kernel, lead),
        grid=(lead + planes,),
        in_specs=[
            pl.BlockSpec((lines, None, res, width), token_block),
            pl.BlockSpec((lines, None, res, width), lambda p: (0, jnp.maximum(p - lead, 0), 0, 0)),
            pl.BlockSpec((res, res), lambda p: (0, 0)),
        ],
        out_specs=pl.BlockSpec((lines * res, width), lambda p: (0, p)),
        out_shape=jax.ShapeDtypeStruct((lines * res, columns), BF16),
        cost_estimate=pl.CostEstimate(
            flops=2 * lines * res * columns * res, bytes_accessed=4 * lines * res * columns, transcendentals=0
        ),
        name="order_sent",
    )(tokens, queries, order)


def project_kernel(x_ref, w_ref, order_ref, *out_refs):
    out = jnp.dot(x_ref[...].reshape(-1, x_ref.shape[-1]), w_ref[...], preferred_element_type=F32)
    out = out.astype(BF16)
    tile = w_ref.shape[1]
    home_ref = out_refs[0]
    home_ref[...] = out.reshape(home_ref.shape)
    if len(out_refs) > 1:
        lines, res, _ = x_ref.shape
        span = res // lines
        by_line = out.reshape(lines, res, tile)
        for i in range(lines):
            rows = by_line[:, i * span : (i + 1) * span].reshape(res, tile)
            out_refs[1][pl.ds(i * res, res), :] = pick(order_ref[...], rows)


def project(tokens, weight, order, plane, sent_width):
    depth, width = weight.shape
    tile = 512
    if tokens.ndim == 4:
        lines, planes, res, _ = tokens.shape
        x_spec = pl.BlockSpec((lines, None, res, depth), lambda n: (0, plane, 0, 0))
        rows = lines * res
        out_specs = [pl.BlockSpec((lines, res, tile), lambda n: (0, 0, n))]
        out_shape = [jax.ShapeDtypeStruct((lines, res, width), BF16)]
    else:
        rows = tokens.shape[0]
        x_spec = pl.BlockSpec((rows, depth), lambda n: (0, plane))
        out_specs = [pl.BlockSpec((rows, tile), lambda n: (0, n))]
        out_shape = [jax.ShapeDtypeStruct((rows, width), BF16)]
    if sent_width:
        out_specs.append(pl.BlockSpec((rows, tile), lambda n: (0, n)))
        out_shape.append(jax.ShapeDtypeStruct((rows, sent_width), BF16))
    return pl.pallas_call(
        project_kernel,
        grid=(width // tile,),
        in_specs=[
            x_spec,
            pl.BlockSpec((depth, tile), lambda n: (0, n)),
            pl.BlockSpec(order.shape, lambda n: (0, 0)),
        ],
        out_specs=out_specs,
        out_shape=out_shape,
        cost_estimate=pl.CostEstimate(
            flops=2 * rows * depth * width,
            bytes_accessed=2 * (rows * (depth + 2 * width) + depth * width),
            transcendentals=0,
        ),
        name=f"project_{plane}",
    )(tokens, weight, order)


def to_away(src_ref, order_ref, dst_ref):
    lines, res, width = dst_ref.shape
    span = res // lines
    for c in range(lines):
        rows = pick(order_ref[...], src_ref[pl.ds(c * res, res), :])
        for pos in range(lines):
            dst_ref[pos, pl.ds(c * span, span), :] = rows[pos * span : (pos + 1) * span]


def attend(q, k, v, bias):
    scores = lax.dot_general(q, k, (((1,), (1,)), ((), ())), preferred_element_type=F32)
    scores = scores * SCALE + bias
    peak = jnp.max(scores, axis=1, keepdims=True)
    weights = jnp.exp(scores - peak)
    total = jnp.sum(weights, axis=1, keepdims=True)
    out = jnp.dot(weights.astype(BF16), v, preferred_element_type=F32)
    return out, peak, total


def far_kernel(moved_kv, column, q_ref, kv_ref, bias_ref, order_ref, back_ref, *rest):
    out_ref, q_s, kv_s, mean_s, sent_s, sem = rest[-6:]
    lines, res, width = q_s.shape
    span = res // lines
    heads = width // HDIM
    to_away(q_ref, order_ref, q_s)
    if moved_kv:
        to_away(kv_ref, order_ref, kv_s)
    else:
        kv_s = kv_ref
    lane = lax.broadcasted_iota(jnp.int32, (res, LANES), 1)

    def step(i, carry):
        lse = jnp.zeros((res, LANES), F32)
        for h in range(heads):
            at = pl.ds(h * HDIM, HDIM)
            out, peak, total = attend(
                q_s[i, :, at], kv_s[i, :, at], kv_s[i, :, pl.ds(width + h * HDIM, HDIM)], bias_ref[...]
            )
            mean_s[i, :, at] = (out * (1.0 / total)).astype(BF16)
            lse = jnp.where(lane == h, peak + jnp.log(total), lse)
        high = lse.astype(BF16).astype(F32)
        mid = (lse - high).astype(BF16).astype(F32)
        low = (lse - high - mid).astype(BF16).astype(F32)
        parts = high + pltpu.roll(mid, 16, 1) + pltpu.roll(low, 32, 1)
        mean_s[i, :, pl.ds(width, LANES)] = parts.astype(BF16)
        return carry

    lax.fori_loop(0, lines, step, 0)
    for c in range(lines):
        rows = jnp.concatenate([mean_s[pos, pl.ds(c * span, span), :] for pos in range(lines)], axis=0)
        sent_s[pl.ds(c * res, res), :] = pick(back_ref[...], rows)
    copy = pltpu.make_async_copy(sent_s, out_ref.at[:, pl.ds(column, width + LANES)], sem)
    copy.start()
    copy.wait()


VMEM_SPEC = pl.BlockSpec(memory_space=pltpu.VMEM)


def attention_cost(lines, res, width):
    return pl.CostEstimate(
        flops=4 * lines * res * res * width,
        bytes_accessed=2 * lines * res * width * 5,
        transcendentals=lines * res * res * (width // HDIM),
    )


def far_attention(moved_q, kv, bias, order, back, plane, lead, lines, res, width, slot=0, slots=1, into=None):
    moved_kv = kv.ndim == 2
    kv_shape = (lines, res, 2 * width) if moved_kv else (1, 16, LANES)
    kv_block = kv.shape[:-1] + (2 * width,)
    column = slot * (width + LANES)
    shape = (lines * res, slots * (width + LANES))
    in_specs = [
        pl.BlockSpec((lines * res, width), lambda n: (0, lead + plane)),
        pl.BlockSpec(kv_block, lambda n: (0,) * kv.ndim),
        pl.BlockSpec((None, res, res), lambda n: (plane, 0, 0)),
        pl.BlockSpec((res, res), lambda n: (0, 0)),
        pl.BlockSpec((res, res), lambda n: (0, 0)),
    ]
    args = (moved_q, kv, bias, order, back)
    if into is not None:
        in_specs.append(pl.BlockSpec(memory_space=pl.ANY))
        args = args + (into,)
    return pl.pallas_call(
        functools.partial(far_kernel, moved_kv, column),
        grid=(1,),
        in_specs=in_specs,
        out_specs=pl.BlockSpec(memory_space=pl.ANY),
        out_shape=jax.ShapeDtypeStruct(shape, BF16),
        scratch_shapes=[
            pltpu.VMEM((lines, res, width), BF16),
            pltpu.VMEM(kv_shape, BF16),
            pltpu.VMEM((lines, res, width + LANES), BF16),
            pltpu.VMEM((lines * res, width + LANES), BF16),
            pltpu.SemaphoreType.DMA,
        ],
        input_output_aliases={} if into is None else {5: 0},
        cost_estimate=attention_cost(lines, res, width),
        name=f"far_{plane}",
    )(*args)


def far_sum(parts):
    return parts + pltpu.roll(parts, LANES - 16, 1) + pltpu.roll(parts, LANES - 32, 1)


def part_kernel(q_ref, kv_ref, bias_ref, order_ref, mean_ref, lse_ref, kv_s):
    lines, res, width = q_ref.shape
    heads = width // HDIM
    if len(kv_ref.shape) == 2:
        to_away(kv_ref, order_ref, kv_s)
    else:
        kv_s = kv_ref
    lane = lax.broadcasted_iota(jnp.int32, (res, LANES), 1)

    def step(i, carry):
        lse = jnp.zeros((res, LANES), F32)
        for h in range(heads):
            at = pl.ds(h * HDIM, HDIM)
            out, peak, total = attend(
                q_ref[i, :, at], kv_s[i, :, at], kv_s[i, :, pl.ds(width + h * HDIM, HDIM)], bias_ref[i]
            )
            mean_ref[i, :, at] = out * (1.0 / total)
            lse = jnp.where(lane == h, peak + jnp.log(total), lse)
        lse_ref[i] = lse
        return carry

    lax.fori_loop(0, lines, step, 0)


def near_part(queries, kv, bias, order, plane):
    lines, planes, res, width = queries.shape
    return pl.pallas_call(
        part_kernel,
        grid=(1,),
        in_specs=[
            pl.BlockSpec((lines, None, res, width), lambda n: (0, plane, 0, 0)),
            pl.BlockSpec(kv.shape, lambda n: (0,) * kv.ndim),
            pl.BlockSpec((None, lines, res, res), lambda n: (plane, 0, 0, 0)),
            pl.BlockSpec((res, res), lambda n: (0, 0)),
        ],
        out_specs=[
            pl.BlockSpec((lines, res, width), lambda n: (0, 0, 0)),
            pl.BlockSpec((lines, res, LANES), lambda n: (0, 0, 0)),
        ],
        out_shape=[
            jax.ShapeDtypeStruct((lines, res, width), F32),
            jax.ShapeDtypeStruct((lines, res, LANES), F32),
        ],
        scratch_shapes=[pltpu.VMEM((lines, res, 2 * width) if kv.ndim == 2 else (1, 16, LANES), BF16)],
        cost_estimate=attention_cost(lines, res, width),
        name=f"near_part_{plane}",
    )(queries, kv, bias, order)


def merge_kernel(far_ref, mean_ref, lse_ref, back_ref, *rest):
    out_ref = rest[-1]
    lines, span, width = mean_ref.shape
    res = lines * span
    far = pick(back_ref[...], far_ref[...])
    far_lse = far_sum(far[:, width:].astype(F32))
    near_lse = lse_ref[...].reshape(res, LANES)
    top = jnp.maximum(near_lse, far_lse)
    near_w = jnp.exp(near_lse - top)
    far_w = jnp.exp(far_lse - top)
    scale = 1.0 / (near_w + far_w)
    near_w = near_w * scale
    far_w = far_w * scale
    for h in range(width // HDIM):
        at = pl.ds(h * HDIM, HDIM)
        near = mean_ref[:, :, at].reshape(res, HDIM)
        far_h = far[:, h * HDIM : (h + 1) * HDIM].astype(F32)
        mixed = near * near_w[:, h : h + 1] + far_h * far_w[:, h : h + 1]
        out_ref[:, :, at] = mixed.astype(BF16).reshape(lines, span, HDIM)


def merge_parts(far, slot, near, back, plane, planes, done):
    mean, lse = near
    lines, res, width = mean.shape
    span = res // lines
    in_specs = [
        pl.BlockSpec((res, width + LANES), lambda c: (c, slot)),
        pl.BlockSpec((lines, span, width), lambda c: (0, c, 0)),
        pl.BlockSpec((lines, span, LANES), lambda c: (0, c, 0)),
        pl.BlockSpec((res, res), lambda c: (0, 0)),
    ]
    args = (far, mean, lse, back)
    if done is not None:
        in_specs.append(pl.BlockSpec(memory_space=pl.ANY))
        args = args + (done,)
    return pl.pallas_call(
        merge_kernel,
        grid=(lines,),
        in_specs=in_specs,
        out_specs=pl.BlockSpec((lines, None, span, width), lambda c: (0, plane, c, 0)),
        out_shape=jax.ShapeDtypeStruct((lines, planes, res, width), BF16),
        input_output_aliases={} if done is None else {4: 0},
        cost_estimate=pl.CostEstimate(
            flops=2 * lines * res * res * width, bytes_accessed=10 * lines * res * width, transcendentals=0
        ),
        name=f"merge_{plane}",
    )(*args)


def mask_bias(codes, res):
    first_kept = (codes % 2 == 1)[..., None]
    second_kept = (codes >= 2)[..., None]
    kept = jnp.where(jnp.arange(res) < res // 2, first_kept, second_kept)
    return jnp.where(kept, 0.0, -jnp.inf).astype(F32)


def exchange(rows):
    return lax.all_to_all(rows, "seq", split_axis=0, concat_axis=0, tiled=True)


def gather_weight(shard, count, sent, codes):
    outer = 1
    while outer * outer < count // 2:
        outer *= 2
    inner = count // outer
    across = [[o * inner + i for o in range(outer)] for i in range(inner)]
    within = [[o * inner + i for i in range(inner)] for o in range(outer)]
    blocks = lax.all_gather(shard[None], "seq", axis=0, tiled=True, axis_index_groups=across)
    blocks, sent, codes = lax.optimization_barrier((blocks, sent, codes))
    blocks = lax.all_gather(blocks, "seq", axis=1, tiled=True, axis_index_groups=within)
    return blocks.reshape(-1, shard.shape[-1]), sent, codes


def on_device(count, tokens, queries, key_weight, value_weight, halves):
    scenes, lines, planes, res, depth = tokens.shape
    width = queries.shape[-1]
    tokens = tokens.reshape(lines, planes, res, depth)
    queries = queries.reshape(lines, planes, res, width)
    halves = halves.reshape(lines, planes, 2, 2)
    to_sent = jnp.asarray(home_order(lines, res), BF16)
    to_home = jnp.asarray(home_order(lines, res).T, BF16)
    away = jnp.asarray(away_order(lines, res), BF16)
    from_away = jnp.asarray(away_order(lines, res).T, BF16)

    dest_half = (np.arange(count) * lines) // (res // 2)
    sent_codes = jnp.where(
        (dest_half == 0)[:, None], halves[:, :, 0, 1].reshape(1, -1), halves[:, :, 1, 1].reshape(1, -1)
    )
    codes = exchange(sent_codes)
    token_planes = 2
    sent = order_sent(tokens, queries, to_sent, token_planes)
    weight, sent, codes = gather_weight(jnp.concatenate([key_weight, value_weight], axis=1), count, sent, codes)
    codes = codes.reshape(res, planes).T
    far_bias = mask_bias(codes, res)
    home_half = jnp.arange(res) // (res // 2)
    near_codes = jnp.where(home_half == 0, halves[:, :, 0:1, 0], halves[:, :, 1:2, 0])
    near_bias = mask_bias(near_codes.transpose(1, 0, 2), res)

    moved = exchange(sent)
    far = functools.partial(
        far_attention, moved, bias=far_bias, order=away, back=from_away,
        lead=token_planes * depth // width, lines=lines, res=res, width=width,
    )
    near = functools.partial(near_part, queries, bias=near_bias, order=away)
    merge = functools.partial(merge_parts, back=to_home, planes=planes)
    home_2, sent_2 = project(tokens, weight, to_sent, 2, 2 * width)
    moved_2 = exchange(sent_2)
    (moved_1,) = project(moved, weight, to_sent, 1, 0)
    (home_0,) = project(tokens, weight, to_sent, 0, 0)
    sent = far(kv=home_2, plane=0, slots=2)
    sent = far(kv=moved_1, plane=2, slot=1, slots=2, into=sent)
    sent, home_0 = lax.optimization_barrier((sent, home_0))
    far_02 = exchange(sent)
    (moved_0,) = project(moved, weight, to_sent, 0, 0)
    near_2 = near(kv=moved_0, plane=2)
    near_1 = near(kv=home_0, plane=1)
    sent, near_1, near_2 = lax.optimization_barrier((far(kv=moved_2, plane=1), near_1, near_2))
    far_1 = exchange(sent)
    (home_1,) = project(tokens, weight, to_sent, 1, 0)
    near_0 = near(kv=home_1, plane=0)
    out = merge(far_02, 0, near_0, plane=0, done=None)
    out = merge(far_02, 1, near_2, plane=2, done=out)
    out = merge(far_1, 0, near_1, plane=1, done=out)
    return out.reshape(scenes, lines, planes, res, width)


def solution(mesh):
    in_specs = (
        P("parts", "seq", None, None, None),
        P("parts", "seq", None, None, None),
        P("seq", None),
        P("seq", None),
        P("parts", "seq", None, None, None),
    )
    return jax.shard_map(
        functools.partial(on_device, mesh.shape["seq"]),
        mesh=mesh,
        in_specs=in_specs,
        out_specs=P("parts", "seq", None, None, None),
        check_vma=False,
    )
```

```python
import functools
import math

import jax
import jax.numpy as jnp
import numpy as np
from jax import lax
from jax.experimental import pallas as pl
from jax.experimental.pallas import tpu as pltpu
from jax.sharding import PartitionSpec as P

HEADS = 12
HDIM = 128
LANES = 128
SCALE = 1.0 / math.sqrt(HDIM)
BF16 = jnp.bfloat16
F32 = jnp.float32


def home_order(lines, res):
    span = res // lines
    out = np.zeros((res, res), np.float32)
    for line in range(lines):
        for dest in range(span // lines):
            for pos in range(lines):
                out[(dest * lines + pos) * lines + line, line * span + dest * lines + pos] = 1.0
    return out


def away_order(lines, res):
    span = res // lines
    out = np.zeros((res, res), np.float32)
    for src in range(span // lines):
        for pos in range(lines):
            for line in range(lines):
                out[pos * span + src * lines + line, (src * lines + pos) * lines + line] = 1.0
    return out


def pick(order, rows):
    return jnp.dot(order, rows, preferred_element_type=F32).astype(BF16)


def order_kernel(lead, tokens_ref, queries_ref, order_ref, out_ref):
    lines, res, width = queries_ref.shape
    span = res // lines
    first = pl.program_id(0) < lead

    def put(ref):
        for i in range(lines):
            rows = ref[:, pl.ds(i * span, span), :].reshape(res, width)
            out_ref[pl.ds(i * res, res), :] = pick(order_ref[...], rows)

    pl.when(first)(lambda: put(tokens_ref))
    pl.when(jnp.logical_not(first))(lambda: put(queries_ref))


def order_sent(tokens, queries, order, token_planes):
    lines, planes, res, width = queries.shape
    depth = tokens.shape[-1]
    parts = depth // width
    lead = token_planes * parts
    columns = (lead + planes) * width

    def token_block(p):
        p = jnp.minimum(p, lead - 1)
        return 0, p // parts, 0, p % parts

    return pl.pallas_call(
        functools.partial(order_kernel, lead),
        grid=(lead + planes,),
        in_specs=[
            pl.BlockSpec((lines, None, res, width), token_block),
            pl.BlockSpec((lines, None, res, width), lambda p: (0, jnp.maximum(p - lead, 0), 0, 0)),
            pl.BlockSpec((res, res), lambda p: (0, 0)),
        ],
        out_specs=pl.BlockSpec((lines * res, width), lambda p: (0, p)),
        out_shape=jax.ShapeDtypeStruct((lines * res, columns), BF16),
        cost_estimate=pl.CostEstimate(
            flops=2 * lines * res * columns * res, bytes_accessed=4 * lines * res * columns, transcendentals=0
        ),
        name="order_sent",
    )(tokens, queries, order)


def project_kernel(parity_ref, x_ref, own_ref, other_ref, order_ref, *out_refs):
    def put(w_ref):
        out = jnp.dot(x_ref[...].reshape(-1, x_ref.shape[-1]), w_ref[...], preferred_element_type=F32)
        out = out.astype(BF16)
        tile = w_ref.shape[1]
        home_ref = out_refs[0]
        home_ref[...] = out.reshape(home_ref.shape)
        if len(out_refs) > 1:
            lines, res, _ = x_ref.shape
            span = res // lines
            by_line = out.reshape(lines, res, tile)
            for i in range(lines):
                rows = by_line[:, i * span : (i + 1) * span].reshape(res, tile)
                out_refs[1][pl.ds(i * res, res), :] = pick(order_ref[...], rows)

    first = pl.program_id(0) < pl.num_programs(0) // 2
    pl.when(first)(lambda: put(own_ref))
    pl.when(jnp.logical_not(first))(lambda: put(other_ref))


def project(tokens, weight, order, plane, sent_width):
    parity, own, other = weight
    depth, half = own.shape
    width = 2 * half
    tile = 512
    steps = half // tile

    def column(n, parity_ref):
        second = (n >= steps).astype(jnp.int32)
        return (parity_ref[0] + second) % 2 * steps + n % steps

    if tokens.ndim == 4:
        lines, planes, res, _ = tokens.shape
        x_spec = pl.BlockSpec((lines, None, res, depth), lambda n, s: (0, plane, 0, 0))
        rows = lines * res
        out_specs = [pl.BlockSpec((lines, res, tile), lambda n, s: (0, 0, column(n, s)))]
        out_shape = [jax.ShapeDtypeStruct((lines, res, width), BF16)]
    else:
        rows = tokens.shape[0]
        x_spec = pl.BlockSpec((rows, depth), lambda n, s: (0, plane))
        out_specs = [pl.BlockSpec((rows, tile), lambda n, s: (0, column(n, s)))]
        out_shape = [jax.ShapeDtypeStruct((rows, width), BF16)]
    if sent_width:
        out_specs.append(pl.BlockSpec((rows, tile), lambda n, s: (0, column(n, s))))
        out_shape.append(jax.ShapeDtypeStruct((rows, sent_width), BF16))
    return pl.pallas_call(
        project_kernel,
        grid_spec=pltpu.PrefetchScalarGridSpec(
            num_scalar_prefetch=1,
            grid=(2 * steps,),
            in_specs=[
                x_spec,
                pl.BlockSpec((depth, tile), lambda n, s: (0, jnp.minimum(n, steps - 1))),
                pl.BlockSpec((depth, tile), lambda n, s: (0, jnp.maximum(n - steps, 0))),
                pl.BlockSpec(order.shape, lambda n, s: (0, 0)),
            ],
            out_specs=out_specs,
        ),
        out_shape=out_shape,
        cost_estimate=pl.CostEstimate(
            flops=2 * rows * depth * width,
            bytes_accessed=2 * (rows * (depth + 2 * width) + depth * width),
            transcendentals=0,
        ),
        name=f"project_{plane}",
    )(parity, tokens, own, other, order)


def to_away(src_ref, order_ref, dst_ref):
    lines, res, width = dst_ref.shape
    span = res // lines
    for c in range(lines):
        rows = pick(order_ref[...], src_ref[pl.ds(c * res, res), :])
        for pos in range(lines):
            dst_ref[pos, pl.ds(c * span, span), :] = rows[pos * span : (pos + 1) * span]


def attend(q, k, v, bias):
    scores = lax.dot_general(q, k, (((1,), (1,)), ((), ())), preferred_element_type=F32)
    scores = scores * SCALE + bias
    peak = jnp.max(scores, axis=1, keepdims=True)
    weights = jnp.exp(scores - peak)
    total = jnp.sum(weights, axis=1, keepdims=True)
    out = jnp.dot(weights.astype(BF16), v, preferred_element_type=F32)
    return out, peak, total


def far_kernel(moved_kv, column, q_ref, kv_ref, bias_ref, order_ref, back_ref, *rest):
    out_ref, q_s, kv_s, mean_s, sent_s, sem = rest[-6:]
    lines, res, width = q_s.shape
    span = res // lines
    heads = width // HDIM
    to_away(q_ref, order_ref, q_s)
    if moved_kv:
        to_away(kv_ref, order_ref, kv_s)
    else:
        kv_s = kv_ref
    lane = lax.broadcasted_iota(jnp.int32, (res, LANES), 1)

    def step(i, carry):
        lse = jnp.zeros((res, LANES), F32)
        for h in range(heads):
            at = pl.ds(h * HDIM, HDIM)
            out, peak, total = attend(
                q_s[i, :, at], kv_s[i, :, at], kv_s[i, :, pl.ds(width + h * HDIM, HDIM)], bias_ref[...]
            )
            mean_s[i, :, at] = (out * (1.0 / total)).astype(BF16)
            lse = jnp.where(lane == h, peak + jnp.log(total), lse)
        high = lse.astype(BF16).astype(F32)
        mid = (lse - high).astype(BF16).astype(F32)
        low = (lse - high - mid).astype(BF16).astype(F32)
        parts = high + pltpu.roll(mid, 16, 1) + pltpu.roll(low, 32, 1)
        mean_s[i, :, pl.ds(width, LANES)] = parts.astype(BF16)
        return carry

    lax.fori_loop(0, lines, step, 0)
    for c in range(lines):
        rows = jnp.concatenate([mean_s[pos, pl.ds(c * span, span), :] for pos in range(lines)], axis=0)
        sent_s[pl.ds(c * res, res), :] = pick(back_ref[...], rows)
    copy = pltpu.make_async_copy(sent_s, out_ref.at[:, pl.ds(column, width + LANES)], sem)
    copy.start()
    copy.wait()


VMEM_SPEC = pl.BlockSpec(memory_space=pltpu.VMEM)


def attention_cost(lines, res, width):
    return pl.CostEstimate(
        flops=4 * lines * res * res * width,
        bytes_accessed=2 * lines * res * width * 5,
        transcendentals=lines * res * res * (width // HDIM),
    )


def far_attention(moved_q, kv, bias, order, back, plane, lead, lines, res, width, slot=0, slots=1, into=None):
    moved_kv = kv.ndim == 2
    kv_shape = (lines, res, 2 * width) if moved_kv else (1, 16, LANES)
    kv_block = kv.shape[:-1] + (2 * width,)
    column = slot * (width + LANES)
    shape = (lines * res, slots * (width + LANES))
    in_specs = [
        pl.BlockSpec((lines * res, width), lambda n: (0, lead + plane)),
        pl.BlockSpec(kv_block, lambda n: (0,) * kv.ndim),
        pl.BlockSpec((None, res, res), lambda n: (plane, 0, 0)),
        pl.BlockSpec((res, res), lambda n: (0, 0)),
        pl.BlockSpec((res, res), lambda n: (0, 0)),
    ]
    args = (moved_q, kv, bias, order, back)
    if into is not None:
        in_specs.append(pl.BlockSpec(memory_space=pl.ANY))
        args = args + (into,)
    return pl.pallas_call(
        functools.partial(far_kernel, moved_kv, column),
        grid=(1,),
        in_specs=in_specs,
        out_specs=pl.BlockSpec(memory_space=pl.ANY),
        out_shape=jax.ShapeDtypeStruct(shape, BF16),
        scratch_shapes=[
            pltpu.VMEM((lines, res, width), BF16),
            pltpu.VMEM(kv_shape, BF16),
            pltpu.VMEM((lines, res, width + LANES), BF16),
            pltpu.VMEM((lines * res, width + LANES), BF16),
            pltpu.SemaphoreType.DMA,
        ],
        input_output_aliases={} if into is None else {5: 0},
        cost_estimate=attention_cost(lines, res, width),
        name=f"far_{plane}",
    )(*args)


def far_sum(parts):
    return parts + pltpu.roll(parts, LANES - 16, 1) + pltpu.roll(parts, LANES - 32, 1)


def part_kernel(q_ref, kv_ref, bias_ref, order_ref, mean_ref, lse_ref, kv_s):
    lines, res, width = q_ref.shape
    heads = width // HDIM
    if len(kv_ref.shape) == 2:
        to_away(kv_ref, order_ref, kv_s)
    else:
        kv_s = kv_ref
    lane = lax.broadcasted_iota(jnp.int32, (res, LANES), 1)

    def step(i, carry):
        lse = jnp.zeros((res, LANES), F32)
        for h in range(heads):
            at = pl.ds(h * HDIM, HDIM)
            out, peak, total = attend(
                q_ref[i, :, at], kv_s[i, :, at], kv_s[i, :, pl.ds(width + h * HDIM, HDIM)], bias_ref[i]
            )
            mean_ref[i, :, at] = out * (1.0 / total)
            lse = jnp.where(lane == h, peak + jnp.log(total), lse)
        lse_ref[i] = lse
        return carry

    lax.fori_loop(0, lines, step, 0)


def near_part(queries, kv, bias, order, plane):
    lines, planes, res, width = queries.shape
    return pl.pallas_call(
        part_kernel,
        grid=(1,),
        in_specs=[
            pl.BlockSpec((lines, None, res, width), lambda n: (0, plane, 0, 0)),
            pl.BlockSpec(kv.shape, lambda n: (0,) * kv.ndim),
            pl.BlockSpec((None, lines, res, res), lambda n: (plane, 0, 0, 0)),
            pl.BlockSpec((res, res), lambda n: (0, 0)),
        ],
        out_specs=[
            pl.BlockSpec((lines, res, width), lambda n: (0, 0, 0)),
            pl.BlockSpec((lines, res, LANES), lambda n: (0, 0, 0)),
        ],
        out_shape=[
            jax.ShapeDtypeStruct((lines, res, width), F32),
            jax.ShapeDtypeStruct((lines, res, LANES), F32),
        ],
        scratch_shapes=[pltpu.VMEM((lines, res, 2 * width) if kv.ndim == 2 else (1, 16, LANES), BF16)],
        cost_estimate=attention_cost(lines, res, width),
        name=f"near_part_{plane}",
    )(queries, kv, bias, order)


def merge_kernel(far_ref, mean_ref, lse_ref, back_ref, *rest):
    out_ref = rest[-1]
    lines, span, width = mean_ref.shape
    res = lines * span
    far = pick(back_ref[...], far_ref[...])
    far_lse = far_sum(far[:, width:].astype(F32))
    near_lse = lse_ref[...].reshape(res, LANES)
    top = jnp.maximum(near_lse, far_lse)
    near_w = jnp.exp(near_lse - top)
    far_w = jnp.exp(far_lse - top)
    scale = 1.0 / (near_w + far_w)
    near_w = near_w * scale
    far_w = far_w * scale
    for h in range(width // HDIM):
        at = pl.ds(h * HDIM, HDIM)
        near = mean_ref[:, :, at].reshape(res, HDIM)
        far_h = far[:, h * HDIM : (h + 1) * HDIM].astype(F32)
        mixed = near * near_w[:, h : h + 1] + far_h * far_w[:, h : h + 1]
        out_ref[:, :, at] = mixed.astype(BF16).reshape(lines, span, HDIM)


def merge_parts(far, slot, near, back, plane, planes, done):
    mean, lse = near
    lines, res, width = mean.shape
    span = res // lines
    in_specs = [
        pl.BlockSpec((res, width + LANES), lambda c: (c, slot)),
        pl.BlockSpec((lines, span, width), lambda c: (0, c, 0)),
        pl.BlockSpec((lines, span, LANES), lambda c: (0, c, 0)),
        pl.BlockSpec((res, res), lambda c: (0, 0)),
    ]
    args = (far, mean, lse, back)
    if done is not None:
        in_specs.append(pl.BlockSpec(memory_space=pl.ANY))
        args = args + (done,)
    return pl.pallas_call(
        merge_kernel,
        grid=(lines,),
        in_specs=in_specs,
        out_specs=pl.BlockSpec((lines, None, span, width), lambda c: (0, plane, c, 0)),
        out_shape=jax.ShapeDtypeStruct((lines, planes, res, width), BF16),
        input_output_aliases={} if done is None else {4: 0},
        cost_estimate=pl.CostEstimate(
            flops=2 * lines * res * res * width, bytes_accessed=10 * lines * res * width, transcendentals=0
        ),
        name=f"merge_{plane}",
    )(*args)


def mask_bias(codes, res):
    first_kept = (codes % 2 == 1)[..., None]
    second_kept = (codes >= 2)[..., None]
    kept = jnp.where(jnp.arange(res) < res // 2, first_kept, second_kept)
    return jnp.where(kept, 0.0, -jnp.inf).astype(F32)


def exchange(rows):
    return lax.all_to_all(rows, "seq", split_axis=0, concat_axis=0, tiled=True)


def gather_weights(key_weight, value_weight, count, sent, codes):
    outer = 1
    while outer * outer < count // 2:
        outer *= 2
    inner = count // outer
    across = [[o * inner + i for o in range(outer)] for i in range(inner)]
    within = [[o * inner + c + i for i in range(0, inner, 2)] for o in range(outer) for c in range(2)]
    swap = [(i, i ^ 1) for i in range(count)]
    even = lax.axis_index("seq") % 2 == 0
    mine = jnp.where(even, key_weight, value_weight)
    got = lax.ppermute(jnp.where(even, value_weight, key_weight), "seq", swap)
    block = jnp.stack([jnp.where(even, mine, got), jnp.where(even, got, mine)])
    block = block.reshape(1, -1, key_weight.shape[-1])
    blocks = lax.all_gather(block, "seq", axis=0, tiled=True, axis_index_groups=across)
    blocks, sent, codes = lax.optimization_barrier((blocks, sent, codes))
    blocks = lax.all_gather(blocks, "seq", axis=1, tiled=True, axis_index_groups=within)
    own = blocks.reshape(-1, key_weight.shape[-1])
    return own, lax.ppermute(own, "seq", swap), sent, codes


def on_device(count, tokens, queries, key_weight, value_weight, halves):
    scenes, lines, planes, res, depth = tokens.shape
    width = queries.shape[-1]
    tokens = tokens.reshape(lines, planes, res, depth)
    queries = queries.reshape(lines, planes, res, width)
    halves = halves.reshape(lines, planes, 2, 2)
    to_sent = jnp.asarray(home_order(lines, res), BF16)
    to_home = jnp.asarray(home_order(lines, res).T, BF16)
    away = jnp.asarray(away_order(lines, res), BF16)
    from_away = jnp.asarray(away_order(lines, res).T, BF16)

    dest_half = (np.arange(count) * lines) // (res // 2)
    sent_codes = jnp.where(
        (dest_half == 0)[:, None], halves[:, :, 0, 1].reshape(1, -1), halves[:, :, 1, 1].reshape(1, -1)
    )
    codes = exchange(sent_codes)
    token_planes = 2
    sent = order_sent(tokens, queries, to_sent, token_planes)
    own, other, sent, codes = gather_weights(key_weight, value_weight, count, sent, codes)
    weight = ((lax.axis_index("seq") % 2).astype(jnp.int32).reshape(1), own, other)
    codes = codes.reshape(res, planes).T
    far_bias = mask_bias(codes, res)
    home_half = jnp.arange(res) // (res // 2)
    near_codes = jnp.where(home_half == 0, halves[:, :, 0:1, 0], halves[:, :, 1:2, 0])
    near_bias = mask_bias(near_codes.transpose(1, 0, 2), res)

    moved = exchange(sent)
    far = functools.partial(
        far_attention, moved, bias=far_bias, order=away, back=from_away,
        lead=token_planes * depth // width, lines=lines, res=res, width=width,
    )
    near = functools.partial(near_part, queries, bias=near_bias, order=away)
    merge = functools.partial(merge_parts, back=to_home, planes=planes)
    home_2, sent_2 = project(tokens, weight, to_sent, 2, 2 * width)
    (home_0,) = project(tokens, weight, to_sent, 0, 0)
    (home_1,) = project(tokens, weight, to_sent, 1, 0)
    sent_2, home_0, home_1 = lax.optimization_barrier((sent_2, home_0, home_1))
    moved_2 = exchange(sent_2)
    (moved_1,) = project(moved, weight, to_sent, 1, 0)
    sent = far(kv=home_2, plane=0, slots=2)
    sent = far(kv=moved_1, plane=2, slot=1, slots=2, into=sent)
    near_1 = near(kv=home_0, plane=1)
    sent, near_1 = lax.optimization_barrier((sent, near_1))
    far_02 = exchange(sent)
    (moved_0,) = project(moved, weight, to_sent, 0, 0)
    near_2 = near(kv=moved_0, plane=2)
    sent, near_2 = lax.optimization_barrier((far(kv=moved_2, plane=1), near_2))
    far_1 = exchange(sent)
    near_0 = near(kv=home_1, plane=0)
    out = merge(far_02, 0, near_0, plane=0, done=None)
    out = merge(far_02, 1, near_2, plane=2, done=out)
    out = merge(far_1, 0, near_1, plane=1, done=out)
    return out.reshape(scenes, lines, planes, res, width)


def solution(mesh):
    in_specs = (
        P("parts", "seq", None, None, None),
        P("parts", "seq", None, None, None),
        P("seq", None),
        P("seq", None),
        P("parts", "seq", None, None, None),
    )
    return jax.shard_map(
        functools.partial(on_device, mesh.shape["seq"]),
        mesh=mesh,
        in_specs=in_specs,
        out_specs=P("parts", "seq", None, None, None),
        check_vma=False,
    )
```

```python
import functools
import math

import jax
import jax.numpy as jnp
import numpy as np
from jax import lax
from jax.experimental import pallas as pl
from jax.experimental.pallas import tpu as pltpu
from jax.sharding import PartitionSpec as P

HEADS = 12
HDIM = 128
LANES = 128
SCALE = 1.0 / math.sqrt(HDIM)
BF16 = jnp.bfloat16
F32 = jnp.float32


def home_order(lines, res):
    span = res // lines
    out = np.zeros((res, res), np.float32)
    for line in range(lines):
        for dest in range(span // lines):
            for pos in range(lines):
                out[(dest * lines + pos) * lines + line, line * span + dest * lines + pos] = 1.0
    return out


def away_order(lines, res):
    span = res // lines
    out = np.zeros((res, res), np.float32)
    for src in range(span // lines):
        for pos in range(lines):
            for line in range(lines):
                out[pos * span + src * lines + line, (src * lines + pos) * lines + line] = 1.0
    return out


def pick(order, rows):
    return jnp.dot(order, rows, preferred_element_type=F32).astype(BF16)


def order_kernel(lead, tokens_ref, queries_ref, order_ref, out_ref):
    lines, res, width = queries_ref.shape
    span = res // lines
    first = pl.program_id(0) < lead

    def put(ref):
        for i in range(lines):
            rows = ref[:, pl.ds(i * span, span), :].reshape(res, width)
            out_ref[pl.ds(i * res, res), :] = pick(order_ref[...], rows)

    pl.when(first)(lambda: put(tokens_ref))
    pl.when(jnp.logical_not(first))(lambda: put(queries_ref))


def order_sent(tokens, queries, order, token_planes):
    lines, planes, res, width = queries.shape
    depth = tokens.shape[-1]
    parts = depth // width
    lead = token_planes * parts
    columns = (lead + planes) * width

    def token_block(p):
        p = jnp.minimum(p, lead - 1)
        return 0, p // parts, 0, p % parts

    return pl.pallas_call(
        functools.partial(order_kernel, lead),
        grid=(lead + planes,),
        in_specs=[
            pl.BlockSpec((lines, None, res, width), token_block),
            pl.BlockSpec((lines, None, res, width), lambda p: (0, jnp.maximum(p - lead, 0), 0, 0)),
            pl.BlockSpec((res, res), lambda p: (0, 0)),
        ],
        out_specs=pl.BlockSpec((lines * res, width), lambda p: (0, p)),
        out_shape=jax.ShapeDtypeStruct((lines * res, columns), BF16),
        cost_estimate=pl.CostEstimate(
            flops=2 * lines * res * columns * res, bytes_accessed=4 * lines * res * columns, transcendentals=0
        ),
        name="order_sent",
    )(tokens, queries, order)


def project_kernel(outs, x_ref, w_ref, order_ref, *rest):
    out_refs = rest[-outs:]
    out = jnp.dot(x_ref[...].reshape(-1, x_ref.shape[-1]), w_ref[...], preferred_element_type=F32)
    out = out.astype(BF16)
    tile = w_ref.shape[1]
    home_ref = out_refs[0]
    home_ref[...] = out.reshape(home_ref.shape)
    if len(out_refs) > 1:
        lines, res, _ = x_ref.shape
        span = res // lines
        by_line = out.reshape(lines, res, tile)
        for i in range(lines):
            rows = by_line[:, i * span : (i + 1) * span].reshape(res, tile)
            out_refs[1][pl.ds(i * res, res), :] = pick(order_ref[...], rows)


def project(tokens, weight, order, plane, sent_width, part=0, parts=1, into=None):
    depth, width = weight.shape
    tile = 512
    steps = width // tile // parts
    skip = part * steps
    if tokens.ndim == 4:
        lines, planes, res, _ = tokens.shape
        x_spec = pl.BlockSpec((lines, None, res, depth), lambda n: (0, plane, 0, 0))
        rows = lines * res
        out_specs = [pl.BlockSpec((lines, res, tile), lambda n: (0, 0, n + skip))]
        out_shape = [jax.ShapeDtypeStruct((lines, res, width), BF16)]
    else:
        rows = tokens.shape[0]
        x_spec = pl.BlockSpec((rows, depth), lambda n: (0, plane))
        out_specs = [pl.BlockSpec((rows, tile), lambda n: (0, n + skip))]
        out_shape = [jax.ShapeDtypeStruct((rows, width), BF16)]
    if sent_width:
        out_specs.append(pl.BlockSpec((rows, tile), lambda n: (0, n)))
        out_shape.append(jax.ShapeDtypeStruct((rows, sent_width), BF16))
    in_specs = [
        x_spec,
        pl.BlockSpec((depth, tile), lambda n: (0, n + skip)),
        pl.BlockSpec(order.shape, lambda n: (0, 0)),
    ]
    args = (tokens, weight, order)
    if into is not None:
        in_specs.append(pl.BlockSpec(memory_space=pl.ANY))
        args = args + (into,)
    return pl.pallas_call(
        functools.partial(project_kernel, len(out_shape)),
        grid=(steps,),
        in_specs=in_specs,
        out_specs=out_specs,
        out_shape=out_shape,
        cost_estimate=pl.CostEstimate(
            flops=2 * rows * depth * width // parts,
            bytes_accessed=2 * (rows * (depth + 2 * width) + depth * width) // parts,
            transcendentals=0,
        ),
        input_output_aliases={} if into is None else {3: 0},
        name=f"project_{plane}",
    )(*args)


def to_away(src_ref, order_ref, dst_ref):
    lines, res, width = dst_ref.shape
    span = res // lines
    for c in range(lines):
        rows = pick(order_ref[...], src_ref[pl.ds(c * res, res), :])
        for pos in range(lines):
            dst_ref[pos, pl.ds(c * span, span), :] = rows[pos * span : (pos + 1) * span]


def attend(q, k, v, bias):
    scores = lax.dot_general(q, k, (((1,), (1,)), ((), ())), preferred_element_type=F32)
    scores = scores * SCALE + bias
    peak = jnp.max(scores, axis=1, keepdims=True)
    weights = jnp.exp(scores - peak)
    total = jnp.sum(weights, axis=1, keepdims=True)
    out = jnp.dot(weights.astype(BF16), v, preferred_element_type=F32)
    return out, peak, total


def far_kernel(moved_kv, column, q_ref, kv_ref, bias_ref, order_ref, back_ref, *rest):
    out_ref, q_s, kv_s, mean_s, sent_s, sem = rest[-6:]
    lines, res, width = q_s.shape
    span = res // lines
    heads = width // HDIM
    to_away(q_ref, order_ref, q_s)
    if moved_kv:
        to_away(kv_ref, order_ref, kv_s)
    else:
        kv_s = kv_ref
    lane = lax.broadcasted_iota(jnp.int32, (res, LANES), 1)

    def step(i, carry):
        lse = jnp.zeros((res, LANES), F32)
        for h in range(heads):
            at = pl.ds(h * HDIM, HDIM)
            out, peak, total = attend(
                q_s[i, :, at], kv_s[i, :, at], kv_s[i, :, pl.ds(width + h * HDIM, HDIM)], bias_ref[...]
            )
            mean_s[i, :, at] = (out * (1.0 / total)).astype(BF16)
            lse = jnp.where(lane == h, peak + jnp.log(total), lse)
        high = lse.astype(BF16).astype(F32)
        mid = (lse - high).astype(BF16).astype(F32)
        low = (lse - high - mid).astype(BF16).astype(F32)
        parts = high + pltpu.roll(mid, 16, 1) + pltpu.roll(low, 32, 1)
        mean_s[i, :, pl.ds(width, LANES)] = parts.astype(BF16)
        return carry

    lax.fori_loop(0, lines, step, 0)
    for c in range(lines):
        rows = jnp.concatenate([mean_s[pos, pl.ds(c * span, span), :] for pos in range(lines)], axis=0)
        sent_s[pl.ds(c * res, res), :] = pick(back_ref[...], rows)
    copy = pltpu.make_async_copy(sent_s, out_ref.at[:, pl.ds(column, width + LANES)], sem)
    copy.start()
    copy.wait()


VMEM_SPEC = pl.BlockSpec(memory_space=pltpu.VMEM)


def attention_cost(lines, res, width):
    return pl.CostEstimate(
        flops=4 * lines * res * res * width,
        bytes_accessed=2 * lines * res * width * 5,
        transcendentals=lines * res * res * (width // HDIM),
    )


def far_attention(moved_q, kv, bias, order, back, plane, lead, lines, res, width, slot=0, slots=1, into=None):
    moved_kv = kv.ndim == 2
    kv_shape = (lines, res, 2 * width) if moved_kv else (1, 16, LANES)
    kv_block = kv.shape[:-1] + (2 * width,)
    column = slot * (width + LANES)
    shape = (lines * res, slots * (width + LANES))
    in_specs = [
        pl.BlockSpec((lines * res, width), lambda n: (0, lead + plane)),
        pl.BlockSpec(kv_block, lambda n: (0,) * kv.ndim),
        pl.BlockSpec((None, res, res), lambda n: (plane, 0, 0)),
        pl.BlockSpec((res, res), lambda n: (0, 0)),
        pl.BlockSpec((res, res), lambda n: (0, 0)),
    ]
    args = (moved_q, kv, bias, order, back)
    if into is not None:
        in_specs.append(pl.BlockSpec(memory_space=pl.ANY))
        args = args + (into,)
    return pl.pallas_call(
        functools.partial(far_kernel, moved_kv, column),
        grid=(1,),
        in_specs=in_specs,
        out_specs=pl.BlockSpec(memory_space=pl.ANY),
        out_shape=jax.ShapeDtypeStruct(shape, BF16),
        scratch_shapes=[
            pltpu.VMEM((lines, res, width), BF16),
            pltpu.VMEM(kv_shape, BF16),
            pltpu.VMEM((lines, res, width + LANES), BF16),
            pltpu.VMEM((lines * res, width + LANES), BF16),
            pltpu.SemaphoreType.DMA,
        ],
        input_output_aliases={} if into is None else {5: 0},
        cost_estimate=attention_cost(lines, res, width),
        name=f"far_{plane}",
    )(*args)


def far_sum(parts):
    return parts + pltpu.roll(parts, LANES - 16, 1) + pltpu.roll(parts, LANES - 32, 1)


def part_kernel(q_ref, kv_ref, bias_ref, order_ref, mean_ref, lse_ref, kv_s):
    _, res, width = q_ref.shape
    lane = lax.broadcasted_iota(jnp.int32, (res, LANES), 1)
    at_line = 0
    if len(kv_ref.shape) == 2:
        at_line = pl.program_id(0)
        pl.when(at_line == 0)(lambda: to_away(kv_ref, order_ref, kv_s))
    else:
        kv_s = kv_ref
    lse = jnp.zeros((res, LANES), F32)
    for h in range(width // HDIM):
        at = pl.ds(h * HDIM, HDIM)
        out, peak, total = attend(
            q_ref[0, :, at], kv_s[at_line, :, at], kv_s[at_line, :, pl.ds(width + h * HDIM, HDIM)], bias_ref[0]
        )
        mean_ref[0, :, at] = out * (1.0 / total)
        lse = jnp.where(lane == h, peak + jnp.log(total), lse)
    lse_ref[0] = lse


def near_part(queries, kv, bias, order, plane):
    lines, planes, res, width = queries.shape
    if kv.ndim == 2:
        kv_spec = pl.BlockSpec(kv.shape, lambda i: (0, 0))
        kv_shape = (lines, res, 2 * width)
    else:
        kv_spec = pl.BlockSpec((1, res, 2 * width), lambda i: (i, 0, 0))
        kv_shape = (1, 16, LANES)
    return pl.pallas_call(
        part_kernel,
        grid=(lines,),
        in_specs=[
            pl.BlockSpec((1, None, res, width), lambda i: (i, plane, 0, 0)),
            kv_spec,
            pl.BlockSpec((None, 1, res, res), lambda i: (plane, i, 0, 0)),
            pl.BlockSpec((res, res), lambda i: (0, 0)),
        ],
        out_specs=[
            pl.BlockSpec((1, res, width), lambda i: (i, 0, 0)),
            pl.BlockSpec((1, res, LANES), lambda i: (i, 0, 0)),
        ],
        out_shape=[
            jax.ShapeDtypeStruct((lines, res, width), F32),
            jax.ShapeDtypeStruct((lines, res, LANES), F32),
        ],
        scratch_shapes=[pltpu.VMEM(kv_shape, BF16)],
        cost_estimate=attention_cost(lines, res, width),
        name=f"near_part_{plane}",
    )(queries, kv, bias, order)


def merge_kernel(far_ref, mean_ref, lse_ref, back_ref, *rest):
    out_ref = rest[-1]
    lines, span, width = mean_ref.shape
    res = lines * span
    far = pick(back_ref[...], far_ref[...])
    far_lse = far_sum(far[:, width:].astype(F32))
    near_lse = lse_ref[...].reshape(res, LANES)
    top = jnp.maximum(near_lse, far_lse)
    near_w = jnp.exp(near_lse - top)
    far_w = jnp.exp(far_lse - top)
    scale = 1.0 / (near_w + far_w)
    near_w = near_w * scale
    far_w = far_w * scale
    for h in range(width // HDIM):
        at = pl.ds(h * HDIM, HDIM)
        near = mean_ref[:, :, at].reshape(res, HDIM)
        far_h = far[:, h * HDIM : (h + 1) * HDIM].astype(F32)
        mixed = near * near_w[:, h : h + 1] + far_h * far_w[:, h : h + 1]
        out_ref[:, :, at] = mixed.astype(BF16).reshape(lines, span, HDIM)


def merge_parts(far, slot, near, back, plane, planes, done):
    mean, lse = near
    lines, res, width = mean.shape
    span = res // lines
    in_specs = [
        pl.BlockSpec((res, width + LANES), lambda c: (c, slot)),
        pl.BlockSpec((lines, span, width), lambda c: (0, c, 0)),
        pl.BlockSpec((lines, span, LANES), lambda c: (0, c, 0)),
        pl.BlockSpec((res, res), lambda c: (0, 0)),
    ]
    args = (far, mean, lse, back)
    if done is not None:
        in_specs.append(pl.BlockSpec(memory_space=pl.ANY))
        args = args + (done,)
    return pl.pallas_call(
        merge_kernel,
        grid=(lines,),
        in_specs=in_specs,
        out_specs=pl.BlockSpec((lines, None, span, width), lambda c: (0, plane, c, 0)),
        out_shape=jax.ShapeDtypeStruct((lines, planes, res, width), BF16),
        input_output_aliases={} if done is None else {4: 0},
        cost_estimate=pl.CostEstimate(
            flops=2 * lines * res * res * width, bytes_accessed=10 * lines * res * width, transcendentals=0
        ),
        name=f"merge_{plane}",
    )(*args)


def mask_bias(codes, res):
    first_kept = (codes % 2 == 1)[..., None]
    second_kept = (codes >= 2)[..., None]
    kept = jnp.where(jnp.arange(res) < res // 2, first_kept, second_kept)
    return jnp.where(kept, 0.0, -jnp.inf).astype(F32)


def exchange(rows):
    return lax.all_to_all(rows, "seq", split_axis=0, concat_axis=0, tiled=True)


def gather_weight(shard, count, sent, codes):
    outer = 1
    while outer * outer < count // 2:
        outer *= 2
    inner = count // outer
    across = [[o * inner + i for o in range(outer)] for i in range(inner)]
    within = [[o * inner + i for i in range(inner)] for o in range(outer)]
    blocks = lax.all_gather(shard[None], "seq", axis=0, tiled=True, axis_index_groups=across)
    blocks, sent, codes = lax.optimization_barrier((blocks, sent, codes))
    blocks = lax.all_gather(blocks, "seq", axis=1, tiled=True, axis_index_groups=within)
    return blocks.reshape(-1, shard.shape[-1]), sent, codes


def on_device(count, tokens, queries, key_weight, value_weight, halves):
    scenes, lines, planes, res, depth = tokens.shape
    width = queries.shape[-1]
    tokens = tokens.reshape(lines, planes, res, depth)
    queries = queries.reshape(lines, planes, res, width)
    halves = halves.reshape(lines, planes, 2, 2)
    to_sent = jnp.asarray(home_order(lines, res), BF16)
    to_home = jnp.asarray(home_order(lines, res).T, BF16)
    away = jnp.asarray(away_order(lines, res), BF16)
    from_away = jnp.asarray(away_order(lines, res).T, BF16)

    dest_half = (np.arange(count) * lines) // (res // 2)
    sent_codes = jnp.where(
        (dest_half == 0)[:, None], halves[:, :, 0, 1].reshape(1, -1), halves[:, :, 1, 1].reshape(1, -1)
    )
    codes = exchange(sent_codes)
    token_planes = 2
    sent = order_sent(tokens, queries, to_sent, token_planes)
    weight, sent, codes = gather_weight(jnp.concatenate([key_weight, value_weight], axis=1), count, sent, codes)
    codes = codes.reshape(res, planes).T
    far_bias = mask_bias(codes, res)
    home_half = jnp.arange(res) // (res // 2)
    near_codes = jnp.where(home_half == 0, halves[:, :, 0:1, 0], halves[:, :, 1:2, 0])
    near_bias = mask_bias(near_codes.transpose(1, 0, 2), res)

    moved = exchange(sent)
    far = functools.partial(
        far_attention, moved, bias=far_bias, order=away, back=from_away,
        lead=token_planes * depth // width, lines=lines, res=res, width=width,
    )
    near = functools.partial(near_part, queries, bias=near_bias, order=away)
    merge = functools.partial(merge_parts, back=to_home, planes=planes)
    home_2, sent_2 = project(tokens, weight, to_sent, 2, 2 * width)
    moved_2 = exchange(sent_2)
    (moved_1,) = project(moved, weight, to_sent, 1, 0)
    (home_0,) = project(tokens, weight, to_sent, 0, 0)
    sent = far(kv=home_2, plane=0, slots=2)
    sent = far(kv=moved_1, plane=2, slot=1, slots=2, into=sent)
    sent, home_0 = lax.optimization_barrier((sent, home_0))
    far_02 = exchange(sent)
    (moved_0,) = project(moved, weight, to_sent, 0, 0)
    near_2 = near(kv=moved_0, plane=2)
    near_1 = near(kv=home_0, plane=1)
    (home_1,) = project(tokens, weight, to_sent, 1, 0, 0, 2)
    sent, near_1, near_2, home_1 = lax.optimization_barrier((far(kv=moved_2, plane=1), near_1, near_2, home_1))
    far_1 = exchange(sent)
    (home_1,) = project(tokens, weight, to_sent, 1, 0, 1, 2, home_1)
    near_0 = near(kv=home_1, plane=0)
    out = merge(far_02, 0, near_0, plane=0, done=None)
    out = merge(far_02, 1, near_2, plane=2, done=out)
    out = merge(far_1, 0, near_1, plane=1, done=out)
    return out.reshape(scenes, lines, planes, res, width)


def solution(mesh):
    in_specs = (
        P("parts", "seq", None, None, None),
        P("parts", "seq", None, None, None),
        P("seq", None),
        P("seq", None),
        P("parts", "seq", None, None, None),
    )
    return jax.shard_map(
        functools.partial(on_device, mesh.shape["seq"]),
        mesh=mesh,
        in_specs=in_specs,
        out_specs=P("parts", "seq", None, None, None),
        check_vma=False,
    )
```

```python
import functools
import math

import jax
import jax.numpy as jnp
import numpy as np
from jax import lax
from jax.experimental import pallas as pl
from jax.experimental.pallas import tpu as pltpu
from jax.sharding import PartitionSpec as P

HEADS = 12
HDIM = 128
LANES = 128
SCALE = 1.0 / math.sqrt(HDIM)
BF16 = jnp.bfloat16
F32 = jnp.float32


def home_order(lines, res):
    span = res // lines
    out = np.zeros((res, res), np.float32)
    for line in range(lines):
        for dest in range(span // lines):
            for pos in range(lines):
                out[(dest * lines + pos) * lines + line, line * span + dest * lines + pos] = 1.0
    return out


def away_order(lines, res):
    span = res // lines
    out = np.zeros((res, res), np.float32)
    for src in range(span // lines):
        for pos in range(lines):
            for line in range(lines):
                out[pos * span + src * lines + line, (src * lines + pos) * lines + line] = 1.0
    return out


def pick(order, rows):
    return jnp.dot(order, rows, preferred_element_type=F32).astype(BF16)


def order_kernel(lead, tokens_ref, queries_ref, order_ref, out_ref):
    lines, res, width = queries_ref.shape
    span = res // lines
    first = pl.program_id(0) < lead

    def put(ref):
        for i in range(lines):
            rows = ref[:, pl.ds(i * span, span), :].reshape(res, width)
            out_ref[pl.ds(i * res, res), :] = pick(order_ref[...], rows)

    pl.when(first)(lambda: put(tokens_ref))
    pl.when(jnp.logical_not(first))(lambda: put(queries_ref))


def order_sent(tokens, queries, order, token_planes):
    lines, planes, res, width = queries.shape
    depth = tokens.shape[-1]
    parts = depth // width
    lead = token_planes * parts
    columns = (lead + planes) * width

    def token_block(p):
        p = jnp.minimum(p, lead - 1)
        return 0, p // parts, 0, p % parts

    return pl.pallas_call(
        functools.partial(order_kernel, lead),
        grid=(lead + planes,),
        in_specs=[
            pl.BlockSpec((lines, None, res, width), token_block),
            pl.BlockSpec((lines, None, res, width), lambda p: (0, jnp.maximum(p - lead, 0), 0, 0)),
            pl.BlockSpec((res, res), lambda p: (0, 0)),
        ],
        out_specs=pl.BlockSpec((lines * res, width), lambda p: (0, p)),
        out_shape=jax.ShapeDtypeStruct((lines * res, columns), BF16),
        cost_estimate=pl.CostEstimate(
            flops=2 * lines * res * columns * res, bytes_accessed=4 * lines * res * columns, transcendentals=0
        ),
        name="order_sent",
    )(tokens, queries, order)


def project_kernel(outs, x_ref, w_ref, order_ref, *rest):
    out_refs = rest[-outs:]
    out = jnp.dot(x_ref[...].reshape(-1, x_ref.shape[-1]), w_ref[...], preferred_element_type=F32)
    out = out.astype(BF16)
    tile = w_ref.shape[1]
    home_ref = out_refs[0]
    home_ref[...] = out.reshape(home_ref.shape)
    if len(out_refs) > 1:
        lines, res, _ = x_ref.shape
        span = res // lines
        by_line = out.reshape(lines, res, tile)
        for i in range(lines):
            rows = by_line[:, i * span : (i + 1) * span].reshape(res, tile)
            out_refs[1][pl.ds(i * res, res), :] = pick(order_ref[...], rows)


def project(tokens, weight, order, plane, sent_width, part=0, parts=1, into=None):
    depth, width = weight.shape
    tile = 512
    steps = width // tile // parts
    skip = part * steps
    if tokens.ndim == 4:
        lines, planes, res, _ = tokens.shape
        x_spec = pl.BlockSpec((lines, None, res, depth), lambda n: (0, plane, 0, 0))
        rows = lines * res
        out_specs = [pl.BlockSpec((lines, res, tile), lambda n: (0, 0, n + skip))]
        out_shape = [jax.ShapeDtypeStruct((lines, res, width), BF16)]
    else:
        rows = tokens.shape[0]
        x_spec = pl.BlockSpec((rows, depth), lambda n: (0, plane))
        out_specs = [pl.BlockSpec((rows, tile), lambda n: (0, n + skip))]
        out_shape = [jax.ShapeDtypeStruct((rows, width), BF16)]
    if sent_width:
        out_specs.append(pl.BlockSpec((rows, tile), lambda n: (0, n)))
        out_shape.append(jax.ShapeDtypeStruct((rows, sent_width), BF16))
    in_specs = [
        x_spec,
        pl.BlockSpec((depth, tile), lambda n: (0, n + skip)),
        pl.BlockSpec(order.shape, lambda n: (0, 0)),
    ]
    args = (tokens, weight, order)
    if into is not None:
        in_specs.append(pl.BlockSpec(memory_space=pl.ANY))
        args = args + (into,)
    return pl.pallas_call(
        functools.partial(project_kernel, len(out_shape)),
        grid=(steps,),
        in_specs=in_specs,
        out_specs=out_specs,
        out_shape=out_shape,
        cost_estimate=pl.CostEstimate(
            flops=2 * rows * depth * width // parts,
            bytes_accessed=2 * (rows * (depth + 2 * width) + depth * width) // parts,
            transcendentals=0,
        ),
        input_output_aliases={} if into is None else {3: 0},
        name=f"project_{plane}",
    )(*args)


def to_away(src_ref, order_ref, dst_ref):
    lines, res, width = dst_ref.shape
    span = res // lines
    for c in range(lines):
        rows = pick(order_ref[...], src_ref[pl.ds(c * res, res), :])
        for pos in range(lines):
            dst_ref[pos, pl.ds(c * span, span), :] = rows[pos * span : (pos + 1) * span]


def attend(q, k, v, bias):
    scores = lax.dot_general(q, k, (((1,), (1,)), ((), ())), preferred_element_type=F32)
    scores = scores * SCALE + bias
    peak = jnp.max(scores, axis=1, keepdims=True)
    weights = jnp.exp(scores - peak)
    total = jnp.sum(weights, axis=1, keepdims=True)
    out = jnp.dot(weights.astype(BF16), v, preferred_element_type=F32)
    return out, peak, total


def far_kernel(moved_kv, column, q_ref, kv_ref, bias_ref, order_ref, back_ref, *rest):
    out_ref, q_s, kv_s, mean_s, sent_s, sem = rest[-6:]
    lines, res, width = q_s.shape
    span = res // lines
    heads = width // HDIM
    to_away(q_ref, order_ref, q_s)
    if moved_kv:
        to_away(kv_ref, order_ref, kv_s)
    else:
        kv_s = kv_ref
    lane = lax.broadcasted_iota(jnp.int32, (res, LANES), 1)

    def step(i, carry):
        lse = jnp.zeros((res, LANES), F32)
        for h in range(heads):
            at = pl.ds(h * HDIM, HDIM)
            out, peak, total = attend(
                q_s[i, :, at], kv_s[i, :, at], kv_s[i, :, pl.ds(width + h * HDIM, HDIM)], bias_ref[...]
            )
            mean_s[i, :, at] = (out * (1.0 / total)).astype(BF16)
            lse = jnp.where(lane == h, peak + jnp.log(total), lse)
        high = lse.astype(BF16).astype(F32)
        mid = (lse - high).astype(BF16).astype(F32)
        low = (lse - high - mid).astype(BF16).astype(F32)
        parts = high + pltpu.roll(mid, 16, 1) + pltpu.roll(low, 32, 1)
        mean_s[i, :, pl.ds(width, LANES)] = parts.astype(BF16)
        return carry

    lax.fori_loop(0, lines, step, 0)
    for c in range(lines):
        rows = jnp.concatenate([mean_s[pos, pl.ds(c * span, span), :] for pos in range(lines)], axis=0)
        sent_s[pl.ds(c * res, res), :] = pick(back_ref[...], rows)
    copy = pltpu.make_async_copy(sent_s, out_ref.at[:, pl.ds(column, width + LANES)], sem)
    copy.start()
    copy.wait()


VMEM_SPEC = pl.BlockSpec(memory_space=pltpu.VMEM)


def attention_cost(lines, res, width):
    return pl.CostEstimate(
        flops=4 * lines * res * res * width,
        bytes_accessed=2 * lines * res * width * 5,
        transcendentals=lines * res * res * (width // HDIM),
    )


def far_attention(moved_q, kv, bias, order, back, plane, lead, lines, res, width, slot=0, slots=1, into=None):
    moved_kv = kv.ndim == 2
    kv_shape = (lines, res, 2 * width) if moved_kv else (1, 16, LANES)
    kv_block = kv.shape[:-1] + (2 * width,)
    column = slot * (width + LANES)
    shape = (lines * res, slots * (width + LANES))
    in_specs = [
        pl.BlockSpec((lines * res, width), lambda n: (0, lead + plane)),
        pl.BlockSpec(kv_block, lambda n: (0,) * kv.ndim),
        pl.BlockSpec((None, res, res), lambda n: (plane, 0, 0)),
        pl.BlockSpec((res, res), lambda n: (0, 0)),
        pl.BlockSpec((res, res), lambda n: (0, 0)),
    ]
    args = (moved_q, kv, bias, order, back)
    if into is not None:
        in_specs.append(pl.BlockSpec(memory_space=pl.ANY))
        args = args + (into,)
    return pl.pallas_call(
        functools.partial(far_kernel, moved_kv, column),
        grid=(1,),
        in_specs=in_specs,
        out_specs=pl.BlockSpec(memory_space=pl.ANY),
        out_shape=jax.ShapeDtypeStruct(shape, BF16),
        scratch_shapes=[
            pltpu.VMEM((lines, res, width), BF16),
            pltpu.VMEM(kv_shape, BF16),
            pltpu.VMEM((lines, res, width + LANES), BF16),
            pltpu.VMEM((lines * res, width + LANES), BF16),
            pltpu.SemaphoreType.DMA,
        ],
        input_output_aliases={} if into is None else {5: 0},
        cost_estimate=attention_cost(lines, res, width),
        name=f"far_{plane}",
    )(*args)


def far_sum(parts):
    return parts + pltpu.roll(parts, LANES - 16, 1) + pltpu.roll(parts, LANES - 32, 1)


def part_kernel(q_ref, kv_ref, bias_ref, order_ref, mean_ref, lse_ref, kv_s):
    _, res, width = q_ref.shape
    lane = lax.broadcasted_iota(jnp.int32, (res, LANES), 1)
    at_line = 0
    if len(kv_ref.shape) == 2:
        at_line = pl.program_id(0)
        pl.when(at_line == 0)(lambda: to_away(kv_ref, order_ref, kv_s))
    else:
        kv_s = kv_ref
    lse = jnp.zeros((res, LANES), F32)
    for h in range(width // HDIM):
        at = pl.ds(h * HDIM, HDIM)
        out, peak, total = attend(
            q_ref[0, :, at], kv_s[at_line, :, at], kv_s[at_line, :, pl.ds(width + h * HDIM, HDIM)], bias_ref[0]
        )
        mean_ref[0, :, at] = out * (1.0 / total)
        lse = jnp.where(lane == h, peak + jnp.log(total), lse)
    lse_ref[0] = lse


def near_part(queries, kv, bias, order, plane):
    lines, planes, res, width = queries.shape
    if kv.ndim == 2:
        kv_spec = pl.BlockSpec(kv.shape, lambda i: (0, 0))
        kv_shape = (lines, res, 2 * width)
    else:
        kv_spec = pl.BlockSpec((1, res, 2 * width), lambda i: (i, 0, 0))
        kv_shape = (1, 16, LANES)
    return pl.pallas_call(
        part_kernel,
        grid=(lines,),
        in_specs=[
            pl.BlockSpec((1, None, res, width), lambda i: (i, plane, 0, 0)),
            kv_spec,
            pl.BlockSpec((None, 1, res, res), lambda i: (plane, i, 0, 0)),
            pl.BlockSpec((res, res), lambda i: (0, 0)),
        ],
        out_specs=[
            pl.BlockSpec((1, res, width), lambda i: (i, 0, 0)),
            pl.BlockSpec((1, res, LANES), lambda i: (i, 0, 0)),
        ],
        out_shape=[
            jax.ShapeDtypeStruct((lines, res, width), F32),
            jax.ShapeDtypeStruct((lines, res, LANES), F32),
        ],
        scratch_shapes=[pltpu.VMEM(kv_shape, BF16)],
        cost_estimate=attention_cost(lines, res, width),
        name=f"near_part_{plane}",
    )(queries, kv, bias, order)


def merge_kernel(far_ref, mean_ref, lse_ref, back_ref, *rest):
    out_ref = rest[-1]
    lines, span, width = mean_ref.shape
    res = lines * span
    far = pick(back_ref[...], far_ref[...])
    far_lse = far_sum(far[:, width:].astype(F32))
    near_lse = lse_ref[...].reshape(res, LANES)
    top = jnp.maximum(near_lse, far_lse)
    near_w = jnp.exp(near_lse - top)
    far_w = jnp.exp(far_lse - top)
    near_w = near_w * (1.0 / (near_w + far_w))
    for h in range(width // HDIM):
        at = pl.ds(h * HDIM, HDIM)
        near = mean_ref[:, :, at].reshape(res, HDIM)
        far_h = far[:, h * HDIM : (h + 1) * HDIM].astype(F32)
        mixed = far_h + (near - far_h) * near_w[:, h : h + 1]
        out_ref[:, :, at] = mixed.astype(BF16).reshape(lines, span, HDIM)


def merge_parts(far, slot, near, back, plane, planes, done):
    mean, lse = near
    lines, res, width = mean.shape
    span = res // lines
    in_specs = [
        pl.BlockSpec((res, width + LANES), lambda c: (c, slot)),
        pl.BlockSpec((lines, span, width), lambda c: (0, c, 0)),
        pl.BlockSpec((lines, span, LANES), lambda c: (0, c, 0)),
        pl.BlockSpec((res, res), lambda c: (0, 0)),
    ]
    args = (far, mean, lse, back)
    if done is not None:
        in_specs.append(pl.BlockSpec(memory_space=pl.ANY))
        args = args + (done,)
    return pl.pallas_call(
        merge_kernel,
        grid=(lines,),
        in_specs=in_specs,
        out_specs=pl.BlockSpec((lines, None, span, width), lambda c: (0, plane, c, 0)),
        out_shape=jax.ShapeDtypeStruct((lines, planes, res, width), BF16),
        input_output_aliases={} if done is None else {4: 0},
        cost_estimate=pl.CostEstimate(
            flops=2 * lines * res * res * width, bytes_accessed=10 * lines * res * width, transcendentals=0
        ),
        name=f"merge_{plane}",
    )(*args)


def mask_bias(codes, res):
    first_kept = (codes % 2 == 1)[..., None]
    second_kept = (codes >= 2)[..., None]
    kept = jnp.where(jnp.arange(res) < res // 2, first_kept, second_kept)
    return jnp.where(kept, 0.0, -jnp.inf).astype(F32)


def exchange(rows):
    return lax.all_to_all(rows, "seq", split_axis=0, concat_axis=0, tiled=True)


def gather_weight(shard, count, sent, codes):
    outer = 1
    while outer * outer < count // 2:
        outer *= 2
    inner = count // outer
    across = [[o * inner + i for o in range(outer)] for i in range(inner)]
    within = [[o * inner + i for i in range(inner)] for o in range(outer)]
    blocks = lax.all_gather(shard[None], "seq", axis=0, tiled=True, axis_index_groups=across)
    blocks, sent, codes = lax.optimization_barrier((blocks, sent, codes))
    blocks = lax.all_gather(blocks, "seq", axis=1, tiled=True, axis_index_groups=within)
    return blocks.reshape(-1, shard.shape[-1]), sent, codes


def on_device(count, tokens, queries, key_weight, value_weight, halves):
    scenes, lines, planes, res, depth = tokens.shape
    width = queries.shape[-1]
    tokens = tokens.reshape(lines, planes, res, depth)
    queries = queries.reshape(lines, planes, res, width)
    halves = halves.reshape(lines, planes, 2, 2)
    to_sent = jnp.asarray(home_order(lines, res), BF16)
    to_home = jnp.asarray(home_order(lines, res).T, BF16)
    away = jnp.asarray(away_order(lines, res), BF16)
    from_away = jnp.asarray(away_order(lines, res).T, BF16)

    dest_half = (np.arange(count) * lines) // (res // 2)
    sent_codes = jnp.where(
        (dest_half == 0)[:, None], halves[:, :, 0, 1].reshape(1, -1), halves[:, :, 1, 1].reshape(1, -1)
    )
    codes = exchange(sent_codes)
    token_planes = 2
    sent = order_sent(tokens, queries, to_sent, token_planes)
    weight, sent, codes = gather_weight(jnp.concatenate([key_weight, value_weight], axis=1), count, sent, codes)
    codes = codes.reshape(res, planes).T
    far_bias = mask_bias(codes, res)
    home_half = jnp.arange(res) // (res // 2)
    near_codes = jnp.where(home_half == 0, halves[:, :, 0:1, 0], halves[:, :, 1:2, 0])
    near_bias = mask_bias(near_codes.transpose(1, 0, 2), res)

    moved = exchange(sent)
    far = functools.partial(
        far_attention, moved, bias=far_bias, order=away, back=from_away,
        lead=token_planes * depth // width, lines=lines, res=res, width=width,
    )
    near = functools.partial(near_part, queries, bias=near_bias, order=away)
    merge = functools.partial(merge_parts, back=to_home, planes=planes)
    home_2, sent_2 = project(tokens, weight, to_sent, 2, 2 * width)
    moved_2 = exchange(sent_2)
    (moved_1,) = project(moved, weight, to_sent, 1, 0)
    (home_0,) = project(tokens, weight, to_sent, 0, 0)
    sent = far(kv=home_2, plane=0, slots=2)
    sent = far(kv=moved_1, plane=2, slot=1, slots=2, into=sent)
    sent, home_0 = lax.optimization_barrier((sent, home_0))
    far_02 = exchange(sent)
    (moved_0,) = project(moved, weight, to_sent, 0, 0)
    near_2 = near(kv=moved_0, plane=2)
    near_1 = near(kv=home_0, plane=1)
    (home_1,) = project(tokens, weight, to_sent, 1, 0, 0, 2)
    sent, near_1, near_2, home_1 = lax.optimization_barrier((far(kv=moved_2, plane=1), near_1, near_2, home_1))
    far_1 = exchange(sent)
    (home_1,) = project(tokens, weight, to_sent, 1, 0, 1, 2, home_1)
    near_0 = near(kv=home_1, plane=0)
    out = merge(far_02, 0, near_0, plane=0, done=None)
    out = merge(far_02, 1, near_2, plane=2, done=out)
    out = merge(far_1, 0, near_1, plane=1, done=out)
    return out.reshape(scenes, lines, planes, res, width)


def solution(mesh):
    in_specs = (
        P("parts", "seq", None, None, None),
        P("parts", "seq", None, None, None),
        P("seq", None),
        P("seq", None),
        P("parts", "seq", None, None, None),
    )
    return jax.shard_map(
        functools.partial(on_device, mesh.shape["seq"]),
        mesh=mesh,
        in_specs=in_specs,
        out_specs=P("parts", "seq", None, None, None),
        check_vma=False,
    )
```

```python
import functools
import math

import jax
import jax.numpy as jnp
import numpy as np
from jax import lax
from jax.experimental import pallas as pl
from jax.experimental.pallas import tpu as pltpu
from jax.sharding import PartitionSpec as P

HEADS = 12
HDIM = 128
LANES = 128
SCALE = 1.0 / math.sqrt(HDIM)
BF16 = jnp.bfloat16
F32 = jnp.float32


def home_order(lines, res):
    span = res // lines
    out = np.zeros((res, res), np.float32)
    for line in range(lines):
        for dest in range(span // lines):
            for pos in range(lines):
                out[(dest * lines + pos) * lines + line, line * span + dest * lines + pos] = 1.0
    return out


def away_order(lines, res):
    span = res // lines
    out = np.zeros((res, res), np.float32)
    for src in range(span // lines):
        for pos in range(lines):
            for line in range(lines):
                out[pos * span + src * lines + line, (src * lines + pos) * lines + line] = 1.0
    return out


def pick(order, rows):
    return jnp.dot(order, rows, preferred_element_type=F32).astype(BF16)


def order_kernel(lead, tokens_ref, queries_ref, order_ref, out_ref):
    lines, res, width = queries_ref.shape
    span = res // lines
    first = pl.program_id(0) < lead

    def put(ref):
        for i in range(lines):
            rows = ref[:, pl.ds(i * span, span), :].reshape(res, width)
            out_ref[pl.ds(i * res, res), :] = pick(order_ref[...], rows)

    pl.when(first)(lambda: put(tokens_ref))
    pl.when(jnp.logical_not(first))(lambda: put(queries_ref))


def order_sent(tokens, queries, order, token_planes):
    lines, planes, res, width = queries.shape
    depth = tokens.shape[-1]
    parts = depth // width
    lead = token_planes * parts
    columns = (lead + planes) * width

    def token_block(p):
        p = jnp.minimum(p, lead - 1)
        return 0, p // parts, 0, p % parts

    return pl.pallas_call(
        functools.partial(order_kernel, lead),
        grid=(lead + planes,),
        in_specs=[
            pl.BlockSpec((lines, None, res, width), token_block),
            pl.BlockSpec((lines, None, res, width), lambda p: (0, jnp.maximum(p - lead, 0), 0, 0)),
            pl.BlockSpec((res, res), lambda p: (0, 0)),
        ],
        out_specs=pl.BlockSpec((lines * res, width), lambda p: (0, p)),
        out_shape=jax.ShapeDtypeStruct((lines * res, columns), BF16),
        cost_estimate=pl.CostEstimate(
            flops=2 * lines * res * columns * res, bytes_accessed=4 * lines * res * columns, transcendentals=0
        ),
        name="order_sent",
    )(tokens, queries, order)


def project_kernel(outs, x_ref, w_ref, order_ref, *rest):
    out_refs = rest[-outs:]
    out = jnp.dot(x_ref[...].reshape(-1, x_ref.shape[-1]), w_ref[...], preferred_element_type=F32)
    out = out.astype(BF16)
    tile = w_ref.shape[1]
    home_ref = out_refs[0]
    home_ref[...] = out.reshape(home_ref.shape)
    if len(out_refs) > 1:
        lines, res, _ = x_ref.shape
        span = res // lines
        by_line = out.reshape(lines, res, tile)
        for i in range(lines):
            rows = by_line[:, i * span : (i + 1) * span].reshape(res, tile)
            out_refs[1][pl.ds(i * res, res), :] = pick(order_ref[...], rows)


def project(tokens, weight, order, plane, sent_width, part=0, parts=1, into=None):
    depth, width = weight.shape
    tile = 512
    steps = width // tile // parts
    skip = part * steps
    if tokens.ndim == 4:
        lines, planes, res, _ = tokens.shape
        x_spec = pl.BlockSpec((lines, None, res, depth), lambda n: (0, plane, 0, 0))
        rows = lines * res
        out_specs = [pl.BlockSpec((lines, res, tile), lambda n: (0, 0, n + skip))]
        out_shape = [jax.ShapeDtypeStruct((lines, res, width), BF16)]
    else:
        rows = tokens.shape[0]
        x_spec = pl.BlockSpec((rows, depth), lambda n: (0, plane))
        out_specs = [pl.BlockSpec((rows, tile), lambda n: (0, n + skip))]
        out_shape = [jax.ShapeDtypeStruct((rows, width), BF16)]
    if sent_width:
        out_specs.append(pl.BlockSpec((rows, tile), lambda n: (0, n)))
        out_shape.append(jax.ShapeDtypeStruct((rows, sent_width), BF16))
    in_specs = [
        x_spec,
        pl.BlockSpec((depth, tile), lambda n: (0, n + skip)),
        pl.BlockSpec(order.shape, lambda n: (0, 0)),
    ]
    args = (tokens, weight, order)
    if into is not None:
        in_specs.append(pl.BlockSpec(memory_space=pl.ANY))
        args = args + (into,)
    return pl.pallas_call(
        functools.partial(project_kernel, len(out_shape)),
        grid=(steps,),
        in_specs=in_specs,
        out_specs=out_specs,
        out_shape=out_shape,
        cost_estimate=pl.CostEstimate(
            flops=2 * rows * depth * width // parts,
            bytes_accessed=2 * (rows * (depth + 2 * width) + depth * width) // parts,
            transcendentals=0,
        ),
        input_output_aliases={} if into is None else {3: 0},
        name=f"project_{plane}",
    )(*args)


def to_away(src_ref, order_ref, dst_ref):
    lines, res, width = dst_ref.shape
    span = res // lines
    for c in range(lines):
        rows = pick(order_ref[...], src_ref[pl.ds(c * res, res), :])
        for pos in range(lines):
            dst_ref[pos, pl.ds(c * span, span), :] = rows[pos * span : (pos + 1) * span]


def attend(q, k, v, bias):
    scores = lax.dot_general(q, k, (((1,), (1,)), ((), ())), preferred_element_type=F32)
    scores = scores * SCALE + bias
    peak = jnp.max(scores, axis=1, keepdims=True)
    weights = jnp.exp(scores - peak)
    total = jnp.sum(weights, axis=1, keepdims=True)
    out = jnp.dot(weights.astype(BF16), v, preferred_element_type=F32)
    return out, peak, total


def far_kernel(moved_kv, column, q_ref, kv_ref, bias_ref, order_ref, back_ref, *rest):
    out_ref, q_s, kv_s, mean_s, sent_s, sem = rest[-6:]
    lines, res, width = q_s.shape
    span = res // lines
    heads = width // HDIM
    to_away(q_ref, order_ref, q_s)
    if moved_kv:
        to_away(kv_ref, order_ref, kv_s)
    else:
        kv_s = kv_ref
    lane = lax.broadcasted_iota(jnp.int32, (res, LANES), 1)

    def step(i, carry):
        peaks, totals = jnp.zeros((res, LANES), F32), jnp.ones((res, LANES), F32)
        for h in range(heads):
            at = pl.ds(h * HDIM, HDIM)
            out, peak, total = attend(
                q_s[i, :, at], kv_s[i, :, at], kv_s[i, :, pl.ds(width + h * HDIM, HDIM)], bias_ref[...]
            )
            mean_s[i, :, at] = (out * (1.0 / total)).astype(BF16)
            peaks = jnp.where(lane == h, peak, peaks)
            totals = jnp.where(lane == h, total, totals)
        lse = peaks + jnp.log(totals)
        high = lse.astype(BF16).astype(F32)
        mid = (lse - high).astype(BF16).astype(F32)
        low = (lse - high - mid).astype(BF16).astype(F32)
        parts = high + pltpu.roll(mid, 16, 1) + pltpu.roll(low, 32, 1)
        mean_s[i, :, pl.ds(width, LANES)] = parts.astype(BF16)
        return carry

    lax.fori_loop(0, lines, step, 0)
    for c in range(lines):
        rows = jnp.concatenate([mean_s[pos, pl.ds(c * span, span), :] for pos in range(lines)], axis=0)
        sent_s[pl.ds(c * res, res), :] = pick(back_ref[...], rows)
    copy = pltpu.make_async_copy(sent_s, out_ref.at[:, pl.ds(column, width + LANES)], sem)
    copy.start()
    copy.wait()


VMEM_SPEC = pl.BlockSpec(memory_space=pltpu.VMEM)


def attention_cost(lines, res, width):
    return pl.CostEstimate(
        flops=4 * lines * res * res * width,
        bytes_accessed=2 * lines * res * width * 5,
        transcendentals=lines * res * res * (width // HDIM),
    )


def far_attention(moved_q, kv, bias, order, back, plane, lead, lines, res, width, slot=0, slots=1, into=None):
    moved_kv = kv.ndim == 2
    kv_shape = (lines, res, 2 * width) if moved_kv else (1, 16, LANES)
    kv_block = kv.shape[:-1] + (2 * width,)
    column = slot * (width + LANES)
    shape = (lines * res, slots * (width + LANES))
    in_specs = [
        pl.BlockSpec((lines * res, width), lambda n: (0, lead + plane)),
        pl.BlockSpec(kv_block, lambda n: (0,) * kv.ndim),
        pl.BlockSpec((None, res, res), lambda n: (plane, 0, 0)),
        pl.BlockSpec((res, res), lambda n: (0, 0)),
        pl.BlockSpec((res, res), lambda n: (0, 0)),
    ]
    args = (moved_q, kv, bias, order, back)
    if into is not None:
        in_specs.append(pl.BlockSpec(memory_space=pl.ANY))
        args = args + (into,)
    return pl.pallas_call(
        functools.partial(far_kernel, moved_kv, column),
        grid=(1,),
        in_specs=in_specs,
        out_specs=pl.BlockSpec(memory_space=pl.ANY),
        out_shape=jax.ShapeDtypeStruct(shape, BF16),
        scratch_shapes=[
            pltpu.VMEM((lines, res, width), BF16),
            pltpu.VMEM(kv_shape, BF16),
            pltpu.VMEM((lines, res, width + LANES), BF16),
            pltpu.VMEM((lines * res, width + LANES), BF16),
            pltpu.SemaphoreType.DMA,
        ],
        input_output_aliases={} if into is None else {5: 0},
        cost_estimate=attention_cost(lines, res, width),
        name=f"far_{plane}",
    )(*args)


def far_sum(parts):
    return parts + pltpu.roll(parts, LANES - 16, 1) + pltpu.roll(parts, LANES - 32, 1)


def part_kernel(q_ref, kv_ref, bias_ref, order_ref, mean_ref, lse_ref, kv_s):
    _, res, width = q_ref.shape
    lane = lax.broadcasted_iota(jnp.int32, (res, LANES), 1)
    at_line = 0
    if len(kv_ref.shape) == 2:
        at_line = pl.program_id(0)
        pl.when(at_line == 0)(lambda: to_away(kv_ref, order_ref, kv_s))
    else:
        kv_s = kv_ref
    peaks, totals = jnp.zeros((res, LANES), F32), jnp.ones((res, LANES), F32)
    for h in range(width // HDIM):
        at = pl.ds(h * HDIM, HDIM)
        out, peak, total = attend(
            q_ref[0, :, at], kv_s[at_line, :, at], kv_s[at_line, :, pl.ds(width + h * HDIM, HDIM)], bias_ref[0]
        )
        mean_ref[0, :, at] = out * (1.0 / total)
        peaks = jnp.where(lane == h, peak, peaks)
        totals = jnp.where(lane == h, total, totals)
    lse_ref[0] = peaks + jnp.log(totals)


def near_part(queries, kv, bias, order, plane):
    lines, planes, res, width = queries.shape
    if kv.ndim == 2:
        kv_spec = pl.BlockSpec(kv.shape, lambda i: (0, 0))
        kv_shape = (lines, res, 2 * width)
    else:
        kv_spec = pl.BlockSpec((1, res, 2 * width), lambda i: (i, 0, 0))
        kv_shape = (1, 16, LANES)
    return pl.pallas_call(
        part_kernel,
        grid=(lines,),
        in_specs=[
            pl.BlockSpec((1, None, res, width), lambda i: (i, plane, 0, 0)),
            kv_spec,
            pl.BlockSpec((None, 1, res, res), lambda i: (plane, i, 0, 0)),
            pl.BlockSpec((res, res), lambda i: (0, 0)),
        ],
        out_specs=[
            pl.BlockSpec((1, res, width), lambda i: (i, 0, 0)),
            pl.BlockSpec((1, res, LANES), lambda i: (i, 0, 0)),
        ],
        out_shape=[
            jax.ShapeDtypeStruct((lines, res, width), F32),
            jax.ShapeDtypeStruct((lines, res, LANES), F32),
        ],
        scratch_shapes=[pltpu.VMEM(kv_shape, BF16)],
        cost_estimate=attention_cost(lines, res, width),
        name=f"near_part_{plane}",
    )(queries, kv, bias, order)


def merge_kernel(far_ref, mean_ref, lse_ref, back_ref, *rest):
    out_ref = rest[-1]
    lines, span, width = mean_ref.shape
    res = lines * span
    far = pick(back_ref[...], far_ref[...])
    far_lse = far_sum(far[:, width:].astype(F32))
    near_lse = lse_ref[...].reshape(res, LANES)
    top = jnp.maximum(near_lse, far_lse)
    near_w = jnp.exp(near_lse - top)
    far_w = jnp.exp(far_lse - top)
    near_w = near_w * (1.0 / (near_w + far_w))
    for h in range(width // HDIM):
        at = pl.ds(h * HDIM, HDIM)
        near = mean_ref[:, :, at].reshape(res, HDIM)
        far_h = far[:, h * HDIM : (h + 1) * HDIM].astype(F32)
        mixed = far_h + (near - far_h) * near_w[:, h : h + 1]
        out_ref[:, :, at] = mixed.astype(BF16).reshape(lines, span, HDIM)


def merge_parts(far, slot, near, back, plane, planes, done):
    mean, lse = near
    lines, res, width = mean.shape
    span = res // lines
    in_specs = [
        pl.BlockSpec((res, width + LANES), lambda c: (c, slot)),
        pl.BlockSpec((lines, span, width), lambda c: (0, c, 0)),
        pl.BlockSpec((lines, span, LANES), lambda c: (0, c, 0)),
        pl.BlockSpec((res, res), lambda c: (0, 0)),
    ]
    args = (far, mean, lse, back)
    if done is not None:
        in_specs.append(pl.BlockSpec(memory_space=pl.ANY))
        args = args + (done,)
    return pl.pallas_call(
        merge_kernel,
        grid=(lines,),
        in_specs=in_specs,
        out_specs=pl.BlockSpec((lines, None, span, width), lambda c: (0, plane, c, 0)),
        out_shape=jax.ShapeDtypeStruct((lines, planes, res, width), BF16),
        input_output_aliases={} if done is None else {4: 0},
        cost_estimate=pl.CostEstimate(
            flops=2 * lines * res * res * width, bytes_accessed=10 * lines * res * width, transcendentals=0
        ),
        name=f"merge_{plane}",
    )(*args)


def mask_bias(codes, res):
    first_kept = (codes % 2 == 1)[..., None]
    second_kept = (codes >= 2)[..., None]
    kept = jnp.where(jnp.arange(res) < res // 2, first_kept, second_kept)
    return jnp.where(kept, 0.0, -jnp.inf).astype(F32)


def exchange(rows):
    return lax.all_to_all(rows, "seq", split_axis=0, concat_axis=0, tiled=True)


def gather_weight(shard, count, sent, codes):
    outer = 1
    while outer * outer < count // 2:
        outer *= 2
    inner = count // outer
    across = [[o * inner + i for o in range(outer)] for i in range(inner)]
    within = [[o * inner + i for i in range(inner)] for o in range(outer)]
    blocks = lax.all_gather(shard[None], "seq", axis=0, tiled=True, axis_index_groups=across)
    blocks, sent, codes = lax.optimization_barrier((blocks, sent, codes))
    blocks = lax.all_gather(blocks, "seq", axis=1, tiled=True, axis_index_groups=within)
    return blocks.reshape(-1, shard.shape[-1]), sent, codes


def on_device(count, tokens, queries, key_weight, value_weight, halves):
    scenes, lines, planes, res, depth = tokens.shape
    width = queries.shape[-1]
    tokens = tokens.reshape(lines, planes, res, depth)
    queries = queries.reshape(lines, planes, res, width)
    halves = halves.reshape(lines, planes, 2, 2)
    to_sent = jnp.asarray(home_order(lines, res), BF16)
    to_home = jnp.asarray(home_order(lines, res).T, BF16)
    away = jnp.asarray(away_order(lines, res), BF16)
    from_away = jnp.asarray(away_order(lines, res).T, BF16)

    dest_half = (np.arange(count) * lines) // (res // 2)
    sent_codes = jnp.where(
        (dest_half == 0)[:, None], halves[:, :, 0, 1].reshape(1, -1), halves[:, :, 1, 1].reshape(1, -1)
    )
    codes = exchange(sent_codes)
    token_planes = 2
    sent = order_sent(tokens, queries, to_sent, token_planes)
    weight, sent, codes = gather_weight(jnp.concatenate([key_weight, value_weight], axis=1), count, sent, codes)
    codes = codes.reshape(res, planes).T
    far_bias = mask_bias(codes, res)
    home_half = jnp.arange(res) // (res // 2)
    near_codes = jnp.where(home_half == 0, halves[:, :, 0:1, 0], halves[:, :, 1:2, 0])
    near_bias = mask_bias(near_codes.transpose(1, 0, 2), res)

    moved = exchange(sent)
    far = functools.partial(
        far_attention, moved, bias=far_bias, order=away, back=from_away,
        lead=token_planes * depth // width, lines=lines, res=res, width=width,
    )
    near = functools.partial(near_part, queries, bias=near_bias, order=away)
    merge = functools.partial(merge_parts, back=to_home, planes=planes)
    home_2, sent_2 = project(tokens, weight, to_sent, 2, 2 * width)
    moved_2 = exchange(sent_2)
    (moved_1,) = project(moved, weight, to_sent, 1, 0)
    (home_0,) = project(tokens, weight, to_sent, 0, 0)
    sent = far(kv=home_2, plane=0, slots=2)
    sent = far(kv=moved_1, plane=2, slot=1, slots=2, into=sent)
    sent, home_0 = lax.optimization_barrier((sent, home_0))
    far_02 = exchange(sent)
    (moved_0,) = project(moved, weight, to_sent, 0, 0)
    near_2 = near(kv=moved_0, plane=2)
    near_1 = near(kv=home_0, plane=1)
    (home_1,) = project(tokens, weight, to_sent, 1, 0, 0, 2)
    sent, near_1, near_2, home_1 = lax.optimization_barrier((far(kv=moved_2, plane=1), near_1, near_2, home_1))
    far_1 = exchange(sent)
    (home_1,) = project(tokens, weight, to_sent, 1, 0, 1, 2, home_1)
    near_0 = near(kv=home_1, plane=0)
    out = merge(far_02, 0, near_0, plane=0, done=None)
    out = merge(far_02, 1, near_2, plane=2, done=out)
    out = merge(far_1, 0, near_1, plane=1, done=out)
    return out.reshape(scenes, lines, planes, res, width)


def solution(mesh):
    in_specs = (
        P("parts", "seq", None, None, None),
        P("parts", "seq", None, None, None),
        P("seq", None),
        P("seq", None),
        P("parts", "seq", None, None, None),
    )
    return jax.shard_map(
        functools.partial(on_device, mesh.shape["seq"]),
        mesh=mesh,
        in_specs=in_specs,
        out_specs=P("parts", "seq", None, None, None),
        check_vma=False,
    )
```
